128 devices in a mesh: dp: 2 (over core), vocab: 64 (over y, z, x).
Axes of the slice: x: 4, y: 4, z: 4, core: 2. Of those that a mesh axis runs over, the one named last changes fastest.
Arguments:
- mentor_score_matrix: bfloat16 [512, 122880], P('dp', 'vocab'), may hold values from -12 to 512
- learner_score_matrix: bfloat16 [512, 262144], P('dp', 'vocab'), may hold values from -12 to 512
- align_dev: int32 [1920, 2], P('vocab'), may hold values from 0 to 63, all different within a row; in each aligned block of 30 rows (0 to 29, 30 to 59, ...) at most 2 rows name the same one
- align_slot: int32 [1920, 2], P('vocab'), may hold values from 0 to 63
- align_weight: bfloat16 [1920, 2, 4096], P('vocab'), may hold values from 0.00077819824 to 0.015625
Outputs:
- scaled_grad: bfloat16 [512, 262144], P('dp', 'vocab')
- divergence_penalty_result: float32 [], replicated
The draws below stay inside these ranges and needn't reach their ends.
Inputs may be any that keep to these rules, and one draw needn't show every extreme that they name: `align_dev`: the 30 teacher blocks of one vocab shard name each owner at most 2 times in all, and in every draw some shard names some owner exactly 2 times; the 2 owners of one teacher block differ.
All inputs are finite; a program needn't handle non-finite values.
Results may differ from the reference program's by a relative error of at most 0.0039.
Values may be sent and summed in bfloat16 or wider, within the bound.
No kernel may reach another device: no remote copies, remote signals or barrier semaphores. Data moves between devices by JAX's collectives and lax.ppermute only.
A program may use at most 64 MiB of HBM per device.

```python
import math
import jax
import jax.numpy as jnp
import numpy as np
from jax import lax

BLK = 64
TB_DEV = 30
SB_DEV = 64
TOPK = 2
SMOOTHING_HEAT = 2
TB = 1920
SB = 4096
VT = 122880
VS = 262144
SYMBOL_NUMBER = 512
MOST = 2
N_VOCAB = 64


def logit_field(key, row_count, col_count, ramp_low):
    noise_draw = jnp.clip(jax.random.normal(jax.random.fold_in(key, 11), (row_count, col_count), jnp.float32), -4.0, 4.0)
    column_place = jnp.arange(col_count, dtype=jnp.float32)[None, :] / float(col_count)
    return 3.0 * noise_draw + ramp_low * column_place


def draw_mentor_score_matrix(key, part):
    return logit_field(jax.random.fold_in(key, 21), SYMBOL_NUMBER, VT, 3.6).astype(jnp.bfloat16)


def draw_learner_score_matrix(key, part):
    return logit_field(jax.random.fold_in(key, 22), SYMBOL_NUMBER, VS, 0.0).astype(jnp.bfloat16)


def place_ends(entries, own_key, smallest, largest):
    longest = entries.shape.index(max(entries.shape))
    spots = []
    for shift in (0, 1):
        where = [jax.random.randint(jax.random.fold_in(own_key, axis), (), 0, length) for axis, length in enumerate(entries.shape)]
        where[longest] = (where[longest] + shift) % entries.shape[longest]
        spots.append(tuple(where))
    return entries.at[spots[0]].set(smallest).at[spots[1]].set(largest)


def block_scale(stream_key, shape, shards, least, largest):
    factor_of = 1.0
    for axis_at, blocks in shards:
        steps = jax.random.uniform(jax.random.fold_in(jax.random.fold_in(stream_key, 6), axis_at), (blocks,), jnp.float32, least / len(shards), largest / len(shards))
        factor_of = factor_of * jnp.repeat(jnp.exp(steps), shape[axis_at] // blocks).reshape((-1,) + (1,) * (len(shape) - 1 - axis_at))
    return factor_of


def routed_block(rng, own, number, rows, number_of, top, most, skew):
    sequence = jax.random.permutation(rng, number_of)
    crowded, ordinary = shares(number_of, rows * top, most, skew, True), shares(number_of, rows * top, most, skew, False)
    places = jnp.arange(number_of)

    def named(tallies, rotation):
        used = int((tallies > 0).sum())
        fixed = max(1, used // 4)
        moved = fixed + (places - fixed + rotation * (used - fixed)) % max(1, number_of - fixed)
        return jnp.zeros((number_of,), jnp.int32).at[sequence[jnp.where(places < fixed, places, moved)]].set(jnp.asarray(tallies, jnp.int32))

    tallies = jnp.where(number % 4 == 0, named(crowded, number // 4), named(ordinary, number - number // 4 - 1))
    mixed = jax.random.permutation(jax.random.fold_in(own, 3), number_of)
    giver, sink = mixed[0:number_of // 2 * 2:2], mixed[1:number_of // 2 * 2:2]
    slack = jnp.minimum(tallies[giver] - 1, most - tallies[sink]) // 2
    slack = jnp.where((giver == sequence[0]) | (sink == sequence[0]) | (tallies[sink] == 0), 0, jnp.maximum(slack, 0))
    moved = jax.random.randint(jax.random.fold_in(own, 4), (number_of // 2,), 0, 1 << 20) % (slack + 1)
    tallies = tallies.at[giver].add(-moved).at[sink].add(moved)
    items = jnp.searchsorted(jnp.cumsum(tallies), jnp.arange(rows * top), side="right").astype(jnp.int32)
    table = items.reshape(top, rows).T
    table = table[jax.random.permutation(jax.random.fold_in(own, 1), rows)]
    rotation = jax.random.randint(jax.random.fold_in(own, 2), (rows, 1), 0, top)
    return jnp.take_along_axis(table, (jnp.arange(top)[None, :] + rotation) % top, axis=1)


def shares(amount, total, reach, lean, full):
    loads = [(1 << 20) // math.isqrt(grade ** lean) + 1 for grade in range(1, amount + 1)]
    largest = reach if full else min(reach, max(-(-total // amount), total * loads[0] // sum(loads)))
    least = 1 if total - largest >= amount - 1 else 0
    given, surplus = [largest] + [least] * (amount - 1), total - largest - least * (amount - 1)
    while surplus > 0:
        movable = [i for i in range(1, amount) if given[i] < largest] or [i for i in range(1, amount) if given[i] < reach]
        whole, remaining = sum([loads[i] for i in movable]), surplus
        for i in movable:
            extra = min(reach - given[i], max(1, remaining * loads[i] // whole), surplus)
            given[i] = given[i] + extra
            surplus = surplus - extra
    return np.array(given)


def setup_inputs(seed: int = 0) -> dict:
    seeds = jax.random.split(jax.random.key(seed), 6)
    mentor_score_matrix = draw_mentor_score_matrix(jax.random.fold_in(seeds[5], 71), 0)
    learner_score_matrix = draw_learner_score_matrix(jax.random.fold_in(seeds[5], 71), 0)
    align_dev_keys = jax.random.split(jax.random.fold_in(seeds[2], 1), TB // TB_DEV)
    align_dev_turns = jax.random.permutation(jax.random.fold_in(seeds[2], 3), TB // TB_DEV)
    align_dev = jax.vmap(lambda own, number: routed_block(jax.random.fold_in(seeds[2], 2), own, number, TB_DEV, N_VOCAB, TOPK, MOST, 2))(align_dev_keys, align_dev_turns).reshape((TB, TOPK))
    align_slot = place_ends(jax.random.randint(seeds[3], (TB, TOPK), 0, SB_DEV), jax.random.fold_in(seeds[3], 1), 0, SB_DEV - 1).astype(jnp.int32)
    align_weight = jnp.clip(jnp.exp(math.log(0.015625) - 2.9996462 * jax.random.uniform(seeds[4], (TB, TOPK, BLK * BLK), jnp.float32) ** block_scale(seeds[4], (TB, TOPK, BLK * BLK), ((0, 64),), -0.2, 0.2)), 0.00077819824, 0.015625).astype(jnp.bfloat16)
    return {"mentor_score_matrix": mentor_score_matrix, "learner_score_matrix": learner_score_matrix, "align_dev": align_dev, "align_slot": align_slot, "align_weight": align_weight}


def reference(mentor_score_matrix, learner_score_matrix, align_dev, align_slot, align_weight):
    smoothing_heat_value = float(SMOOTHING_HEAT)
    mentor_smoothed_scores = mentor_score_matrix.astype(jnp.float32) / smoothing_heat_value
    teacher_high = jnp.max(mentor_smoothed_scores, axis=1, keepdims=True)
    teacher_lse = teacher_high + jnp.log(jnp.sum(jnp.exp(mentor_smoothed_scores - teacher_high), axis=1, keepdims=True))
    teacher_probs = jnp.exp(mentor_smoothed_scores - teacher_lse).astype(jnp.bfloat16)
    row_count = teacher_probs.shape[0]
    prob_blocks = teacher_probs.astype(jnp.float32).reshape(row_count, TB, BLK)
    weight_blocks = align_weight.astype(jnp.float32).reshape(TB, TOPK, BLK, BLK)
    target_block = (align_dev * SB_DEV + align_slot).astype(jnp.int32)
    target_mass = jnp.zeros((row_count, SB, BLK), jnp.float32)
    for pick_index in range(TOPK):
        contrib = jnp.einsum("rbc,bcd->rbd", prob_blocks, weight_blocks[:, pick_index], precision=lax.Precision.HIGHEST)
        rounded = lax.optimization_barrier(contrib.astype(jnp.bfloat16))
        target_mass = target_mass.at[:, target_block[:, pick_index]].add(rounded.astype(jnp.float32))
    target = target_mass.reshape(row_count, VS)
    target_total = jnp.sum(target, axis=1, keepdims=True)
    learner_smoothed_scores = learner_score_matrix.astype(jnp.float32) / smoothing_heat_value
    student_high = jnp.max(learner_smoothed_scores, axis=1, keepdims=True)
    student_lse = student_high + jnp.log(jnp.sum(jnp.exp(learner_smoothed_scores - student_high), axis=1, keepdims=True))
    student_logprob = learner_smoothed_scores - student_lse
    scaled_grad = (float(VS) * (target_total * jnp.exp(student_logprob) - target)).astype(jnp.bfloat16)
    symbolwise_penalty = jax.scipy.special.xlogy(target, target) - target * student_logprob
    divergence_penalty_result = smoothing_heat_value * smoothing_heat_value * jnp.sum(symbolwise_penalty) / float(SYMBOL_NUMBER)
    return scaled_grad, divergence_penalty_result
```

```python
import functools

import jax
import jax.numpy as jnp
from jax import lax
from jax.experimental import pallas as pl
from jax.experimental.pallas import tpu as pltpu
from jax.sharding import PartitionSpec as P

BLK = 64
LANES = 128
SMOOTHING_HEAT = 2
MOST = 2
STAT_ROWS = 16
TAIL_ROWS = 24

F32 = jnp.float32
BF16 = jnp.bfloat16


def split2(x):
    hi = x.astype(BF16).astype(F32)
    return hi, x - hi


def send_kernel(dev_ref, slot_ref, x_ref, y_ref, w_ref, out_ref, term, tail, cnt, sem, tail_sem):
    rows, width = x_ref.shape
    owners = out_ref.shape[0]
    halves = rows // LANES
    pairs = width // LANES
    student_tiles = y_ref.shape[1] // LANES
    topk = dev_ref.shape[0]
    block_rows = halves * BLK
    inv_heat = 1.0 / SMOOTHING_HEAT

    high = x_ref[:, :LANES]
    for q in range(1, pairs):
        high = jnp.maximum(high, x_ref[:, q * LANES : (q + 1) * LANES])
    teacher_high = jnp.max(high.astype(F32), axis=1, keepdims=True) * inv_heat

    @pl.loop(0, owners)
    def _(i):
        cnt[i] = 0

    lane = lax.broadcasted_iota(jnp.int32, (BLK, LANES), 1)
    even = lane % 2 == 0
    first = lane < BLK
    code_lane = lax.broadcasted_iota(jnp.int32, (8, LANES), 1)
    code = jnp.full((8, LANES), -1.0, F32)
    high_b = jnp.broadcast_to(teacher_high, (rows, LANES))
    exp_sum = jnp.zeros((rows, LANES), F32)
    mass = jnp.zeros((8, rows), F32)
    copies = []
    for q in range(pairs):
        w = w_ref[q * LANES : (q + 1) * LANES, :].astype(F32).T
        a0, a1 = w[:BLK], w[BLK:]
        l0 = jnp.where(even, a0, pltpu.roll(a1, 1, 1))
        l1 = jnp.where(even, pltpu.roll(a0, LANES - 1, 1), a1)
        lhs = jnp.concatenate(
            [
                jnp.where(first, l0, 0.0),
                jnp.where(first, l1, 0.0),
                jnp.where(first, 0.0, l0),
                jnp.where(first, 0.0, l1),
            ],
            axis=0,
        ).astype(BF16)
        e = jnp.exp(x_ref[:, q * LANES : (q + 1) * LANES].astype(F32) * inv_heat - high_b)
        exp_sum = exp_sum + e
        u = lax.dot_general(
            lhs, e.astype(BF16), (((1,), (1,)), ((), ())), preferred_element_type=F32
        ).astype(BF16)
        mass = mass + jnp.sum(u.astype(F32).reshape(4 * BLK // 8, 8, rows), axis=0)
        for edge in range(2 * topk):
            b, k = 2 * q + edge // topk, edge % topk
            index = q * 2 * topk + edge
            for h in range(halves):
                term[index, h * BLK : (h + 1) * BLK, :] = u[
                    edge * BLK : (edge + 1) * BLK, h * LANES : (h + 1) * LANES
                ]
            dst = dev_ref[k, b]
            at = cnt[dst]
            cnt[dst] = at + 1
            code = jnp.where(code_lane == dst * MOST + at, slot_ref[k, b].astype(F32), code)
            copy = pltpu.make_async_copy(
                term.at[index],
                out_ref.at[dst, pl.ds(pl.multiple_of(at * block_rows, block_rows), block_rows), :],
                sem.at[index],
            )
            copy.start()
            copies.append(copy)

    def student_max(t, m):
        return jnp.maximum(m, y_ref[:, pl.ds(pl.multiple_of(t * LANES, LANES), LANES)])

    m = lax.fori_loop(1, student_tiles, student_max, y_ref[:, :LANES])
    student_high = jnp.max(m.astype(F32), axis=1, keepdims=True) * inv_heat
    student_b = jnp.broadcast_to(student_high, (rows, LANES))

    def student_sum(t, s):
        y = y_ref[:, pl.ds(pl.multiple_of(t * LANES, LANES), LANES)].astype(F32)
        return s + jnp.exp(y * inv_heat - student_b)

    student_exp = lax.fori_loop(0, student_tiles, student_sum, jnp.zeros((rows, LANES), F32))

    row_lane = lax.broadcasted_iota(jnp.int32, (rows, LANES), 1)
    teacher_sum = jnp.sum(exp_sum, axis=1, keepdims=True)
    student_sum_ = jnp.sum(student_exp, axis=1, keepdims=True)
    t_hi, t_lo = split2(teacher_sum)
    s_hi, s_lo = split2(student_sum_)
    columns = jnp.zeros((rows, LANES), F32)
    for i, v in ((0, teacher_high), (1, t_hi), (2, t_lo), (5, student_high), (6, s_hi), (7, s_lo)):
        columns = jnp.where(row_lane == i, v, columns)
    r_hi, r_lo = split2(jnp.sum(mass, axis=0, keepdims=True))
    sub = lax.broadcasted_iota(jnp.int32, (8, LANES), 0)
    pieces = []
    for h in range(halves):
        lanes = slice(h * LANES, (h + 1) * LANES)
        s = columns[lanes].T[:8]
        s = jnp.where(sub == 3, r_hi[:, lanes], s)
        pieces.append(jnp.where(sub == 4, r_lo[:, lanes], s))
    stats = jnp.concatenate(pieces, axis=0).astype(BF16)
    codes = code.astype(BF16)

    @pl.loop(0, owners)
    def _(i):
        tail[i, :STAT_ROWS, :] = stats
        tail[i, STAT_ROWS:, :] = codes

    tail_copy = pltpu.make_async_copy(
        tail, out_ref.at[:, pl.ds(MOST * block_rows, TAIL_ROWS), :], tail_sem
    )
    tail_copy.start()
    for copy in copies:
        copy.wait()
    tail_copy.wait()


def receive_kernel(
    arr_ref, y_ref, out_ref, loss_ref, buf, tail, wide, scale, code_v, code_s, acc, lse_b, mass_b,
    sem, tail_sem, code_sem,
):
    owners = arr_ref.shape[0]
    rows, width = y_ref.shape
    halves = rows // LANES
    tiles = width // LANES
    block_rows = halves * BLK
    groups = sem.shape[0]
    per = owners // groups
    inv_heat = 1.0 / SMOOTHING_HEAT
    vocab_width = float(width * owners)
    me = lax.axis_index("vocab")

    tail_copy = pltpu.make_async_copy(
        arr_ref.at[:, pl.ds(MOST * block_rows, TAIL_ROWS), :], tail, tail_sem
    )
    tail_copy.start()

    def block_copy(g):
        return pltpu.make_async_copy(
            arr_ref.at[pl.ds(g * per, per), pl.ds(0, MOST * block_rows), :],
            buf.at[pl.ds(g * per, per)],
            sem.at[g],
        )

    for g in range(groups):
        block_copy(g).start()

    tail_copy.wait()
    wide[...] = tail[...].astype(F32).reshape(owners * TAIL_ROWS, LANES)
    code_v[...] = wide[pl.ds(STAT_ROWS, owners, stride=TAIL_ROWS), :].astype(jnp.int32)
    code_copy = pltpu.make_async_copy(code_v, code_s, code_sem)
    code_copy.start()

    @pl.loop(0, halves * width // 256)
    def _(i):
        acc[pl.ds(pl.multiple_of(i * 256, 256), 256), :] = jnp.zeros((256, LANES), F32)

    for h in range(halves):
        def stat(i):
            return wide[pl.ds(8 * h + i, owners, stride=TAIL_ROWS), :]

        t_high, s_high = stat(0), stat(5)
        t_top = jnp.max(t_high, axis=0, keepdims=True)
        s_top = jnp.max(s_high, axis=0, keepdims=True)
        t_rel = jnp.exp(t_high - t_top)
        inv = 1.0 / jnp.sum(t_rel * (stat(1) + stat(2)), axis=0, keepdims=True)
        scale_h = t_rel * inv
        scale[h * owners : (h + 1) * owners, :] = scale_h
        total = jnp.sum(scale_h * (stat(3) + stat(4)), axis=0, keepdims=True)
        s_sum = jnp.sum(jnp.exp(s_high - s_top) * (stat(6) + stat(7)), axis=0, keepdims=True)
        lse = s_top + jnp.log(s_sum)
        lse_b[h * LANES : (h + 1) * LANES, :] = jnp.broadcast_to(lse, (LANES, LANES)).T
        mass_b[h * LANES : (h + 1) * LANES, :] = (
            jnp.broadcast_to(total, (LANES, LANES)).T * vocab_width
        )

    code_copy.wait()
    for g in range(groups):
        block_copy(g).wait()

        @pl.loop(0, per)
        def _(i):
            src = g * per + i
            for slot in range(MOST):
                c = code_s[src, me * MOST + slot]

                @pl.when(c >= 0)
                def _():
                    for h in range(halves):
                        at = pl.ds(pl.multiple_of(h * width + c * BLK, BLK), BLK)
                        term = buf[src, slot * block_rows + h * BLK : slot * block_rows + (h + 1) * BLK, :]
                        acc[at, :] = acc[at, :] + term.astype(F32) * scale[pl.ds(h * owners + src, 1), :]

    def tile(t, loss):
        cols = pl.ds(pl.multiple_of(t * LANES, LANES), LANES)
        for h in range(halves):
            lanes = slice(h * LANES, (h + 1) * LANES)
            target = acc[pl.ds(pl.multiple_of(h * width + t * LANES, LANES), LANES), :].T
            logprob = y_ref[lanes, cols].astype(F32) * inv_heat - lse_b[lanes, :]
            out_ref[lanes, cols] = (
                mass_b[lanes, :] * jnp.exp(logprob) - vocab_width * target
            ).astype(BF16)
            loss = loss + jnp.where(target > 0.0, target * (jnp.log(target) - logprob), 0.0)
        return loss

    loss = lax.fori_loop(0, tiles, tile, jnp.zeros((LANES, LANES), F32))
    loss_ref[...] = jnp.broadcast_to(
        jnp.sum(loss, axis=0, keepdims=True).reshape(1, 1, LANES), loss_ref.shape
    )


def per_device(mentor_score_matrix, learner_score_matrix, align_dev, align_slot, align_weight):
    owners = lax.axis_size("vocab")
    shards = owners * lax.axis_size("dp")
    rows, teacher_width = mentor_score_matrix.shape
    width = learner_score_matrix.shape[1]
    tb_local, topk = align_dev.shape
    edges = tb_local * topk
    halves = rows // LANES
    block_rows = halves * BLK
    packet_rows = MOST * block_rows + TAIL_ROWS
    chunks = BLK * BLK // LANES
    weight = (
        align_weight.reshape(tb_local, topk, chunks, LANES)
        .transpose(0, 2, 1, 3)
        .reshape(tb_local * chunks * topk, LANES)
    )
    vmem = pl.BlockSpec(memory_space=pltpu.VMEM)
    smem = pl.BlockSpec(memory_space=pltpu.SMEM)
    hbm = pl.BlockSpec(memory_space=pl.ANY)
    outgoing = pl.pallas_call(
        send_kernel,
        out_shape=jax.ShapeDtypeStruct((owners, packet_rows, LANES), BF16),
        in_specs=[smem, smem, vmem, vmem, vmem],
        out_specs=hbm,
        scratch_shapes=[
            pltpu.VMEM((edges, block_rows, LANES), BF16),
            pltpu.VMEM((owners, TAIL_ROWS, LANES), BF16),
            pltpu.SMEM((owners,), jnp.int32),
            pltpu.SemaphoreType.DMA((edges,)),
            pltpu.SemaphoreType.DMA,
        ],
        name="send",
    )(align_dev.T, align_slot.T, mentor_score_matrix, learner_score_matrix, weight)
    arrived = lax.all_to_all(outgoing, "vocab", split_axis=0, concat_axis=0, tiled=True)
    scaled_grad, loss = pl.pallas_call(
        receive_kernel,
        out_shape=(
            jax.ShapeDtypeStruct((rows, width), BF16),
            jax.ShapeDtypeStruct((shards, 1, LANES), F32),
        ),
        in_specs=[hbm, vmem],
        out_specs=(vmem, vmem),
        scratch_shapes=[
            pltpu.VMEM((owners, MOST * block_rows, LANES), BF16),
            pltpu.VMEM((owners, TAIL_ROWS, LANES), BF16),
            pltpu.VMEM((owners * TAIL_ROWS, LANES), F32),
            pltpu.VMEM((halves * owners, LANES), F32),
            pltpu.VMEM((owners, LANES), jnp.int32),
            pltpu.SMEM((owners, LANES), jnp.int32),
            pltpu.VMEM((halves * width, LANES), F32),
            pltpu.VMEM((rows, LANES), F32),
            pltpu.VMEM((rows, LANES), F32),
            pltpu.SemaphoreType.DMA((8,)),
            pltpu.SemaphoreType.DMA,
            pltpu.SemaphoreType.DMA,
        ],
        name="receive",
    )(arrived, learner_score_matrix)
    parts = lax.all_to_all(loss, ("dp", "vocab"), split_axis=0, concat_axis=0, tiled=True)
    tokens = float(rows * lax.axis_size("dp"))
    divergence = SMOOTHING_HEAT * SMOOTHING_HEAT * jnp.sum(parts) / tokens
    return scaled_grad, divergence


def solution(mesh):
    in_specs = (
        P("dp", "vocab"),
        P("dp", "vocab"),
        P("vocab", None),
        P("vocab", None),
        P("vocab", None, None),
    )
    out_specs = (P("dp", "vocab"), P())
    return jax.shard_map(
        per_device, mesh=mesh, in_specs=in_specs, out_specs=out_specs, check_vma=False
    )
```

```python
import math

import jax
import jax.numpy as jnp
from jax import lax
from jax.experimental import pallas as pl
from jax.experimental.pallas import tpu as pltpu
from jax.sharding import PartitionSpec as P

BLK = 64
LANES = 128
SMOOTHING_HEAT = 2
MOST = 2
STAT_ROWS = 16
TAIL_ROWS = 24
EXP2_SCALE = math.log2(math.e) / SMOOTHING_HEAT
TINY = 2.0**-126

F32 = jnp.float32
BF16 = jnp.bfloat16


def split2(x):
    hi = x.astype(BF16).astype(F32)
    return hi, x - hi


def send_kernel(
    dev_ref, slot_ref, x_ref, y_hbm, w_ref, out_ref, y_ref, probs, term, tail, edge_v, pos_v,
    pos_s, sem, tail_sem, y_sem, pos_sem,
):
    rows, width = x_ref.shape
    owners = out_ref.shape[0]
    halves = rows // LANES
    pairs = width // LANES
    student_tiles = y_ref.shape[1] // LANES
    topk, blocks = dev_ref.shape
    block_rows = halves * BLK
    padded = pos_v.shape[0]

    y_copy = pltpu.make_async_copy(y_hbm, y_ref, y_sem)
    y_copy.start()

    edge_v[...] = jnp.full((8, LANES), -1.0, F32)
    edge_v[:topk, :blocks] = dev_ref[...].astype(F32)
    edge_v[topk : 2 * topk, :blocks] = slot_ref[...].astype(F32)
    edge_rows = edge_v[...]
    edge_cols = edge_rows.T[:padded]
    below = lax.broadcasted_iota(jnp.int32, (padded, LANES), 1) < lax.broadcasted_iota(
        jnp.int32, (padded, LANES), 0
    )
    edge_lane = lax.broadcasted_iota(jnp.int32, (padded, LANES), 1)
    code = jnp.zeros((padded, LANES), F32)
    places = jnp.zeros((padded, LANES), F32)
    for k in range(topk):
        owner = edge_cols[:, k : k + 1]
        hits = jnp.zeros((padded, LANES), F32)
        for other in range(topk):
            same = (owner == edge_rows[other : other + 1, :]) & below
            hits = hits + jnp.where(same, 1.0, 0.0)
        place = owner * MOST + jnp.sum(hits, axis=1, keepdims=True)
        code = code + jnp.where(
            place == edge_lane.astype(F32), edge_cols[:, topk + k : topk + k + 1] + 1.0, 0.0
        )
        places = jnp.where(edge_lane == k, place, places)
    codes = jnp.broadcast_to(jnp.sum(code, axis=0, keepdims=True) - 1.0, (8, LANES)).astype(BF16)
    pos_v[...] = places.astype(jnp.int32)
    pos_copy = pltpu.make_async_copy(pos_v, pos_s, pos_sem)
    pos_copy.start()

    def shard_max(ref, h, tiles):
        lanes = slice(h * LANES, (h + 1) * LANES)
        m = ref[lanes, :LANES]
        for t in range(1, tiles):
            m = jnp.maximum(m, ref[lanes, t * LANES : (t + 1) * LANES])
        return jnp.max(m.astype(F32), axis=1, keepdims=True)

    teacher_high, teacher_sum = [], []
    for h in range(halves):
        lanes = slice(h * LANES, (h + 1) * LANES)
        high = shard_max(x_ref, h, pairs)
        high_b = jnp.broadcast_to(high, (LANES, LANES))
        total = jnp.zeros((LANES, LANES), F32)
        for q in range(pairs):
            e = jnp.exp2((x_ref[lanes, q * LANES : (q + 1) * LANES].astype(F32) - high_b) * EXP2_SCALE)
            total = total + e
            probs[q, lanes, :] = e.astype(BF16)
        teacher_high.append(high)
        teacher_sum.append(jnp.sum(total, axis=1, keepdims=True))

    y_copy.wait()
    student_high = [shard_max(y_ref, h, student_tiles) for h in range(halves)]

    lane = lax.broadcasted_iota(jnp.int32, (BLK, LANES), 1)
    even = lane % 2 == 0
    first = lane < BLK
    mass = jnp.zeros((8, rows), F32)
    for q in range(pairs):
        w = w_ref[q * LANES : (q + 1) * LANES, :].astype(F32).T
        a0, a1 = w[:BLK], w[BLK:]
        l0 = jnp.where(even, a0, pltpu.roll(a1, 1, 1))
        l1 = jnp.where(even, pltpu.roll(a0, LANES - 1, 1), a1)
        lhs = jnp.concatenate(
            [
                jnp.where(first, l0, 0.0),
                jnp.where(first, l1, 0.0),
                jnp.where(first, 0.0, l0),
                jnp.where(first, 0.0, l1),
            ],
            axis=0,
        ).astype(BF16)
        u = lax.dot_general(
            lhs, probs[q], (((1,), (1,)), ((), ())), preferred_element_type=F32
        )
        mass = mass + jnp.sum(u.reshape(4 * BLK // 8, 8, rows), axis=0)
        u = u.astype(BF16)
        for edge in range(2 * topk):
            for h in range(halves):
                term[q * 2 * topk + edge, h * BLK : (h + 1) * BLK, :] = u[
                    edge * BLK : (edge + 1) * BLK, h * LANES : (h + 1) * LANES
                ]

    pos_copy.wait()
    copies = []

    def send_edges(lo, hi):
        for index in range(lo, hi):
            place = pos_s[index // topk, index % topk]
            at = pl.multiple_of((place % MOST) * block_rows, block_rows)
            copy = pltpu.make_async_copy(
                term.at[index], out_ref.at[place // MOST, pl.ds(at, block_rows), :], sem.at[index]
            )
            copy.start()
            copies.append(copy)

    edges = blocks * topk
    steps = halves * student_tiles // 4
    student_sum = []
    for h in range(halves):
        lanes = slice(h * LANES, (h + 1) * LANES)
        high_b = jnp.broadcast_to(student_high[h], (LANES, LANES))
        total = jnp.zeros((LANES, LANES), F32)
        for t in range(student_tiles):
            y = y_ref[lanes, t * LANES : (t + 1) * LANES].astype(F32)
            total = total + jnp.exp2((y - high_b) * EXP2_SCALE)
            if t % 4 == 0:
                step = h * student_tiles // 4 + t // 4
                send_edges(edges * step // steps, edges * (step + 1) // steps)
        student_sum.append(jnp.sum(total, axis=1, keepdims=True))

    row_lane = lax.broadcasted_iota(jnp.int32, (LANES, LANES), 1)
    r_hi, r_lo = split2(jnp.sum(mass, axis=0, keepdims=True))
    sub = lax.broadcasted_iota(jnp.int32, (8, LANES), 0)
    pieces = []
    for h in range(halves):
        t_hi, t_lo = split2(teacher_sum[h])
        s_hi, s_lo = split2(student_sum[h])
        columns = jnp.zeros((LANES, LANES), F32)
        for i, v in (
            (0, teacher_high[h]), (1, t_hi), (2, t_lo), (5, student_high[h]), (6, s_hi), (7, s_lo)
        ):
            columns = jnp.where(row_lane == i, v, columns)
        lanes = slice(h * LANES, (h + 1) * LANES)
        s = columns.T[:8]
        s = jnp.where(sub == 3, r_hi[:, lanes], s)
        pieces.append(jnp.where(sub == 4, r_lo[:, lanes], s))
    stats = jnp.concatenate(pieces, axis=0).astype(BF16)
    for i in range(owners):
        tail[i, :STAT_ROWS, :] = stats
        tail[i, STAT_ROWS:, :] = codes
    tail_copy = pltpu.make_async_copy(
        tail, out_ref.at[:, pl.ds(MOST * block_rows, TAIL_ROWS), :], tail_sem
    )
    tail_copy.start()
    for copy in copies:
        copy.wait()
    tail_copy.wait()


def receive_kernel(
    arr_ref, y_hbm, out_hbm, loss_ref, y_ref, out_ref, buf, tail, wide, scale, code_v, code_s, acc,
    bias, mass_b, sem, tail_sem, code_sem, y_sem, out_sem,
):
    owners = arr_ref.shape[0]
    rows, width = y_ref.shape
    halves = rows // LANES
    tiles = width // LANES
    block_rows = halves * BLK
    groups = sem.shape[0]
    per = owners // groups
    span = width + BLK
    vocab_width = float(width * owners)
    me = lax.axis_index("vocab")

    tail_copy = pltpu.make_async_copy(
        arr_ref.at[:, pl.ds(MOST * block_rows, TAIL_ROWS), :], tail, tail_sem
    )
    tail_copy.start()

    def block_copy(g):
        return pltpu.make_async_copy(
            arr_ref.at[pl.ds(g * per, per), pl.ds(0, MOST * block_rows), :],
            buf.at[pl.ds(g * per, per)],
            sem.at[g],
        )

    for g in range(groups):
        block_copy(g).start()
    y_copy = pltpu.make_async_copy(y_hbm, y_ref, y_sem)
    y_copy.start()

    for h in range(halves):

        @pl.loop(0, width // 512)
        def _(i):
            acc[pl.ds(pl.multiple_of(h * span + i * 512, BLK), 512), :] = jnp.zeros((512, LANES), F32)

    tail_copy.wait()
    wide[...] = tail[...].astype(F32).reshape(owners * TAIL_ROWS, LANES)
    codes = wide[pl.ds(STAT_ROWS, owners, stride=TAIL_ROWS), :].astype(jnp.int32)
    code_v[...] = jnp.where(codes < 0, width // BLK, codes)
    code_copy = pltpu.make_async_copy(code_v, code_s, code_sem)
    code_copy.start()

    for h in range(halves):

        def stat(i):
            return wide[pl.ds(8 * h + i, owners, stride=TAIL_ROWS), :]

        t_high, s_high = stat(0), stat(5)
        t_top = jnp.max(t_high, axis=0, keepdims=True)
        s_top = jnp.max(s_high, axis=0, keepdims=True)
        t_rel = jnp.exp2((t_high - t_top) * EXP2_SCALE)
        s_rel = jnp.exp2((s_high - s_top) * EXP2_SCALE)
        inv = vocab_width / jnp.sum(t_rel * (stat(1) + stat(2)), axis=0, keepdims=True)
        scale_h = t_rel * inv
        scale[h * owners : (h + 1) * owners, :] = scale_h
        total = jnp.sum(scale_h * (stat(3) + stat(4)), axis=0, keepdims=True) * (1.0 / vocab_width)
        s_sum = jnp.sum(s_rel * (stat(6) + stat(7)), axis=0, keepdims=True)
        lse = s_top * EXP2_SCALE + jnp.log2(s_sum) - math.log2(vocab_width)
        bias[h * LANES : (h + 1) * LANES, :] = jnp.broadcast_to(lse, (LANES, LANES)).T
        mass_b[h * LANES : (h + 1) * LANES, :] = jnp.broadcast_to(total, (LANES, LANES)).T

    code_copy.wait()
    for g in range(groups):
        block_copy(g).wait()

        def add_source(i, carry):
            src = g * per + i
            for slot in range(MOST):
                c = code_s[src, me * MOST + slot]
                for h in range(halves):
                    at = pl.ds(pl.multiple_of(h * span + c * BLK, BLK), BLK)
                    lo = slot * block_rows + h * BLK
                    term = buf[src, lo : lo + BLK, :].astype(F32)
                    acc[at, :] = acc[at, :] + term * scale[pl.ds(h * owners + src, 1), :]
            return carry

        lax.fori_loop(0, per, add_source, 0, unroll=2)

    y_copy.wait()
    chunks = out_sem.shape[0]
    chunk = width // chunks

    def tile(t, loss):
        cols = pl.ds(pl.multiple_of(t * LANES, LANES), LANES)
        for h in range(halves):
            lanes = slice(h * LANES, (h + 1) * LANES)
            target = acc[pl.ds(pl.multiple_of(h * span + t * LANES, BLK), LANES), :].T
            logprob = y_ref[lanes, cols].astype(F32) * EXP2_SCALE - bias[lanes, :]
            out_ref[lanes, cols] = (mass_b[lanes, :] * jnp.exp2(logprob) - target).astype(BF16)
            term = target * (jnp.log2(jnp.maximum(target, TINY)) - logprob)
            loss = loss + jnp.sum(term.reshape(LANES // 32, 32, LANES), axis=0)
        return loss

    loss = jnp.zeros((32, LANES), F32)
    out_copies = []
    for i in range(chunks):
        per_chunk = tiles // chunks
        loss = lax.fori_loop(i * per_chunk, (i + 1) * per_chunk, tile, loss, unroll=2)
        part = pl.ds(i * chunk, chunk)
        copy = pltpu.make_async_copy(out_ref.at[:, part], out_hbm.at[:, part], out_sem.at[i])
        copy.start()
        out_copies.append(copy)
    loss_ref[...] = jnp.broadcast_to(
        jnp.sum(loss, axis=0, keepdims=True).reshape(1, 1, LANES), loss_ref.shape
    )
    for copy in out_copies:
        copy.wait()


def per_device(mentor_score_matrix, learner_score_matrix, align_dev, align_slot, align_weight):
    owners = lax.axis_size("vocab")
    shards = owners * lax.axis_size("dp")
    rows, teacher_width = mentor_score_matrix.shape
    width = learner_score_matrix.shape[1]
    tb_local, topk = align_dev.shape
    edges = tb_local * topk
    halves = rows // LANES
    block_rows = halves * BLK
    packet_rows = MOST * block_rows + TAIL_ROWS
    chunks = BLK * BLK // LANES
    weight = (
        align_weight.reshape(tb_local, topk, chunks, LANES)
        .transpose(0, 2, 1, 3)
        .reshape(tb_local * chunks * topk, LANES)
    )
    vmem = pl.BlockSpec(memory_space=pltpu.VMEM)
    hbm = pl.BlockSpec(memory_space=pl.ANY)
    outgoing = pl.pallas_call(
        send_kernel,
        out_shape=jax.ShapeDtypeStruct((owners, packet_rows, LANES), BF16),
        in_specs=[vmem, vmem, vmem, hbm, vmem],
        out_specs=hbm,
        scratch_shapes=[
            pltpu.VMEM((rows, width), BF16),
            pltpu.VMEM((teacher_width // LANES, rows, LANES), BF16),
            pltpu.VMEM((edges, block_rows, LANES), BF16),
            pltpu.VMEM((owners, TAIL_ROWS, LANES), BF16),
            pltpu.VMEM((8, LANES), F32),
            pltpu.VMEM((32, LANES), jnp.int32),
            pltpu.SMEM((32, LANES), jnp.int32),
            pltpu.SemaphoreType.DMA((edges,)),
            pltpu.SemaphoreType.DMA,
            pltpu.SemaphoreType.DMA,
            pltpu.SemaphoreType.DMA,
        ],
        name="send",
    )(align_dev.T, align_slot.T, mentor_score_matrix, learner_score_matrix, weight)
    arrived = lax.all_to_all(outgoing, "vocab", split_axis=0, concat_axis=0, tiled=True)
    scaled_grad, loss = pl.pallas_call(
        receive_kernel,
        out_shape=(
            jax.ShapeDtypeStruct((rows, width), BF16),
            jax.ShapeDtypeStruct((shards, 1, LANES), F32),
        ),
        in_specs=[hbm, hbm],
        out_specs=(hbm, vmem),
        scratch_shapes=[
            pltpu.VMEM((rows, width), BF16),
            pltpu.VMEM((rows, width), BF16),
            pltpu.VMEM((owners, MOST * block_rows, LANES), BF16),
            pltpu.VMEM((owners, TAIL_ROWS, LANES), BF16),
            pltpu.VMEM((owners * TAIL_ROWS, LANES), F32),
            pltpu.VMEM((halves * owners, LANES), F32),
            pltpu.VMEM((owners, LANES), jnp.int32),
            pltpu.SMEM((owners, LANES), jnp.int32),
            pltpu.VMEM((halves * (width + BLK), LANES), F32),
            pltpu.VMEM((rows, LANES), F32),
            pltpu.VMEM((rows, LANES), F32),
            pltpu.SemaphoreType.DMA((8,)),
            pltpu.SemaphoreType.DMA,
            pltpu.SemaphoreType.DMA,
            pltpu.SemaphoreType.DMA,
            pltpu.SemaphoreType.DMA((8,)),
        ],
        name="receive",
    )(arrived, learner_score_matrix)
    parts = lax.all_to_all(loss, ("dp", "vocab"), split_axis=0, concat_axis=0, tiled=True)
    tokens = float(rows * lax.axis_size("dp"))
    unit = math.log(2.0) / (width * owners)
    divergence = SMOOTHING_HEAT * SMOOTHING_HEAT * unit / tokens * jnp.sum(parts)
    return scaled_grad, divergence


def solution(mesh):
    in_specs = (
        P("dp", "vocab"),
        P("dp", "vocab"),
        P("vocab", None),
        P("vocab", None),
        P("vocab", None, None),
    )
    out_specs = (P("dp", "vocab"), P())
    return jax.shard_map(
        per_device, mesh=mesh, in_specs=in_specs, out_specs=out_specs, check_vma=False
    )
```

```python
import math

import jax
import jax.numpy as jnp
from jax import lax
from jax.experimental import pallas as pl
from jax.experimental.pallas import tpu as pltpu
from jax.sharding import PartitionSpec as P

BLK = 64
LANES = 128
SMOOTHING_HEAT = 2
MOST = 2
TAIL_ROWS = 16
CODE_ROW = 7
EXP2_SCALE = math.log2(math.e) / SMOOTHING_HEAT
TINY = 2.0**-126

F32 = jnp.float32
BF16 = jnp.bfloat16


def split2(x):
    hi = x.astype(BF16).astype(F32)
    return hi, x - hi


def send_kernel(
    dev_ref, slot_ref, x_ref, y_hbm, w_ref, out_ref, y_ref, probs, high_v, term, tail, edge_v, pos_v,
    pos_s, sem, tail_sem, y_sem, pos_sem,
):
    rows, width = x_ref.shape
    owners = out_ref.shape[0]
    halves = rows // LANES
    pairs = width // LANES
    student_tiles = y_ref.shape[1] // LANES
    topk, blocks = dev_ref.shape
    block_rows = halves * BLK
    padded = pos_v.shape[0]

    y_copy = pltpu.make_async_copy(y_hbm, y_ref, y_sem)
    y_copy.start()

    edge_v[...] = jnp.full((8, LANES), -1.0, F32)
    edge_v[:topk, :blocks] = dev_ref[...].astype(F32)
    edge_v[topk : 2 * topk, :blocks] = slot_ref[...].astype(F32)
    edge_rows = edge_v[...]
    edge_cols = edge_rows.T[:padded]
    below = lax.broadcasted_iota(jnp.int32, (padded, LANES), 1) < lax.broadcasted_iota(
        jnp.int32, (padded, LANES), 0
    )
    edge_lane = lax.broadcasted_iota(jnp.int32, (padded, LANES), 1)
    code = jnp.zeros((padded, LANES), F32)
    places = jnp.zeros((padded, LANES), F32)
    for k in range(topk):
        owner = edge_cols[:, k : k + 1]
        hits = jnp.zeros((padded, LANES), F32)
        for other in range(topk):
            same = (owner == edge_rows[other : other + 1, :]) & below
            hits = hits + jnp.where(same, 1.0, 0.0)
        place = owner * MOST + jnp.sum(hits, axis=1, keepdims=True)
        code = code + jnp.where(
            place == edge_lane.astype(F32), edge_cols[:, topk + k : topk + k + 1] + 1.0, 0.0
        )
        places = jnp.where(edge_lane == k, place, places)
    codes = jnp.sum(code, axis=0, keepdims=True) - 1.0
    pos_v[...] = places.astype(jnp.int32)
    pos_copy = pltpu.make_async_copy(pos_v, pos_s, pos_sem)
    pos_copy.start()

    def shard_max(ref, h, tiles):
        lanes = slice(h * LANES, (h + 1) * LANES)
        m = ref[lanes, :LANES]
        for t in range(1, tiles):
            m = jnp.maximum(m, ref[lanes, t * LANES : (t + 1) * LANES])
        return jnp.max(m.astype(F32), axis=1, keepdims=True)

    teacher_high, teacher_sum = [], []
    for h in range(halves):
        lanes = slice(h * LANES, (h + 1) * LANES)
        high = shard_max(x_ref, h, pairs)
        high_b = jnp.broadcast_to(high, (LANES, LANES))
        total = jnp.zeros((LANES, LANES), F32)
        for q in range(pairs):
            e = jnp.exp2((x_ref[lanes, q * LANES : (q + 1) * LANES].astype(F32) - high_b) * EXP2_SCALE)
            total = total + e
            probs[q, lanes, :] = e.astype(BF16)
        teacher_high.append(high)
        teacher_sum.append(jnp.sum(total, axis=1, keepdims=True))

    y_copy.wait()
    student_high = [shard_max(y_ref, h, student_tiles) for h in range(halves)]

    pos_copy.wait()

    def send_edges(q):
        for index in range(q * 2 * topk, (q + 1) * 2 * topk):
            place = pos_s[index // topk, index % topk]
            at = pl.multiple_of((place % MOST) * block_rows, block_rows)
            pltpu.make_async_copy(
                term.at[index], out_ref.at[place // MOST, pl.ds(at, block_rows), :], sem
            ).start()

    for h in range(halves):
        high_v[h] = jnp.broadcast_to(student_high[h], (LANES, LANES))
    lane = lax.broadcasted_iota(jnp.int32, (BLK, LANES), 1)
    even = lane % 2 == 0
    first = lane < BLK
    mass = jnp.zeros((8, rows), F32)
    student_total = [jnp.zeros((LANES, LANES), F32) for _ in range(halves)]
    items = [(h, t) for h in range(halves) for t in range(student_tiles)]
    for q in range(pairs):
        w = w_ref[q * LANES : (q + 1) * LANES, :].astype(F32).T
        a0, a1 = w[:BLK], w[BLK:]
        l0 = jnp.where(even, a0, pltpu.roll(a1, 1, 1))
        l1 = jnp.where(even, pltpu.roll(a0, LANES - 1, 1), a1)
        lhs = jnp.concatenate(
            [
                jnp.where(first, l0, 0.0),
                jnp.where(first, l1, 0.0),
                jnp.where(first, 0.0, l0),
                jnp.where(first, 0.0, l1),
            ],
            axis=0,
        ).astype(BF16)
        u = lax.dot_general(
            lhs, probs[q], (((1,), (1,)), ((), ())), preferred_element_type=F32
        )
        for h, t in items[len(items) * q // pairs : len(items) * (q + 1) // pairs]:
            y = y_ref[h * LANES : (h + 1) * LANES, t * LANES : (t + 1) * LANES].astype(F32)
            student_total[h] = student_total[h] + jnp.exp2((y - high_v[h]) * EXP2_SCALE)
        mass = mass + jnp.sum(u.reshape(4 * BLK // 8, 8, rows), axis=0)
        u = u.astype(BF16)
        for edge in range(2 * topk):
            for h in range(halves):
                term[q * 2 * topk + edge, h * BLK : (h + 1) * BLK, :] = u[
                    edge * BLK : (edge + 1) * BLK, h * LANES : (h + 1) * LANES
                ]
        if q > 0:
            send_edges(q - 1)
    send_edges(pairs - 1)

    row_lane = lax.broadcasted_iota(jnp.int32, (LANES, LANES), 1)
    r_hi, r_lo = split2(jnp.sum(mass, axis=0, keepdims=True))
    sub = lax.broadcasted_iota(jnp.int32, (8, LANES), 0)
    pieces = []
    for h in range(halves):
        t_hi, t_lo = split2(teacher_sum[h])
        student_sum = jnp.sum(student_total[h], axis=1, keepdims=True)
        s_hi, s_lo = split2(student_high[h] * EXP2_SCALE + jnp.log2(student_sum))
        columns = jnp.zeros((LANES, LANES), F32)
        for i, v in ((0, teacher_high[h]), (1, t_hi), (2, t_lo), (5, s_hi), (6, s_lo)):
            columns = jnp.where(row_lane == i, v, columns)
        lanes = slice(h * LANES, (h + 1) * LANES)
        s = columns.T[:8]
        s = jnp.where(sub == 3, r_hi[:, lanes], s)
        s = jnp.where(sub == 4, r_lo[:, lanes], s)
        pieces.append(jnp.where(sub == CODE_ROW, codes, s))
    stats = jnp.concatenate(pieces, axis=0).astype(BF16)
    for i in range(owners):
        tail[i] = stats
    tail_copy = pltpu.make_async_copy(
        tail, out_ref.at[:, pl.ds(MOST * block_rows, TAIL_ROWS), :], tail_sem
    )
    tail_copy.start()
    pltpu.make_async_copy(term, term, sem).wait()
    tail_copy.wait()


def receive_kernel(
    arr_ref, y_hbm, out_hbm, loss_ref, y_ref, out_ref, buf, tail, wide, scale, code_v, code_s, acc,
    bias, sem, tail_sem, code_sem, y_sem, out_sem,
):
    owners = arr_ref.shape[0]
    rows, width = y_ref.shape
    halves = rows // LANES
    tiles = width // LANES
    block_rows = halves * BLK
    groups = sem.shape[0]
    per = owners // groups
    span = width + BLK
    vocab_width = float(width * owners)
    me = lax.axis_index("vocab")

    tail_copy = pltpu.make_async_copy(
        arr_ref.at[:, pl.ds(MOST * block_rows, TAIL_ROWS), :], tail, tail_sem
    )
    tail_copy.start()

    def block_copy(g):
        return pltpu.make_async_copy(
            arr_ref.at[pl.ds(g * per, per), pl.ds(0, MOST * block_rows), :],
            buf.at[pl.ds(g * per, per)],
            sem.at[g],
        )

    for g in range(groups):
        block_copy(g).start()
    y_copy = pltpu.make_async_copy(y_hbm, y_ref, y_sem)
    y_copy.start()

    for h in range(halves):

        @pl.loop(0, width // 512)
        def _(i):
            acc[pl.ds(pl.multiple_of(h * span + i * 512, BLK), 512), :] = jnp.full((512, LANES), TINY, F32)

    tail_copy.wait()
    wide[...] = tail[...].astype(F32).reshape(owners * TAIL_ROWS, LANES)
    codes = wide[pl.ds(CODE_ROW, owners, stride=TAIL_ROWS), :].astype(jnp.int32)
    code_v[...] = jnp.where(codes < 0, width // BLK, codes)
    code_copy = pltpu.make_async_copy(code_v, code_s, code_sem)
    code_copy.start()

    row_terms = jnp.zeros((1, LANES), F32)
    for h in range(halves):

        def stat(i):
            return wide[pl.ds(8 * h + i, owners, stride=TAIL_ROWS), :]

        t_high = stat(0)
        t_top = jnp.max(t_high, axis=0, keepdims=True)
        t_rel = jnp.exp2((t_high - t_top) * EXP2_SCALE)
        inv = vocab_width / jnp.sum(t_rel * (stat(1) + stat(2)), axis=0, keepdims=True)
        scale_h = t_rel * inv
        scale[h * owners : (h + 1) * owners, :] = scale_h
        total = jnp.sum(scale_h * (stat(3) + stat(4)), axis=0, keepdims=True)
        log_total = jnp.log2(total)
        s_lse = stat(5) + stat(6)
        s_top = jnp.max(s_lse, axis=0, keepdims=True)
        lse = s_top + jnp.log2(jnp.sum(jnp.exp2(s_lse - s_top), axis=0, keepdims=True))
        bias[h * LANES : (h + 1) * LANES, :] = jnp.broadcast_to(lse - log_total, (LANES, LANES)).T
        row_terms = row_terms + total * (log_total - math.log2(vocab_width)) * (1.0 / owners)

    code_copy.wait()
    for g in range(groups):
        block_copy(g).wait()

        def add_source(i, carry):
            src = g * per + i
            for slot in range(MOST):
                c = code_s[src, me * MOST + slot]
                for h in range(halves):
                    at = pl.ds(pl.multiple_of(h * span + c * BLK, BLK), BLK)
                    lo = slot * block_rows + h * BLK
                    term = buf[src, lo : lo + BLK, :].astype(F32)
                    acc[at, :] = acc[at, :] + term * scale[pl.ds(h * owners + src, 1), :]
            return carry

        lax.fori_loop(0, per, add_source, 0, unroll=2)

    y_copy.wait()
    chunks = out_sem.shape[0]
    chunk = width // chunks

    def tile(t, loss):
        cols = pl.ds(pl.multiple_of(t * LANES, LANES), LANES)
        for h in range(halves):
            lanes = slice(h * LANES, (h + 1) * LANES)
            target = acc[pl.ds(pl.multiple_of(h * span + t * LANES, BLK), LANES), :].T
            goal = y_ref[lanes, cols].astype(F32) * EXP2_SCALE - bias[lanes, :]
            out_ref[lanes, cols] = (jnp.exp2(goal) - target).astype(BF16)
            term = target * (jnp.log2(target) - goal)
            loss = loss + jnp.sum(term.reshape(LANES // 32, 32, LANES), axis=0)
        return loss

    loss = jnp.zeros((32, LANES), F32)
    out_copies = []
    for i in range(chunks):
        per_chunk = tiles // chunks
        loss = lax.fori_loop(i * per_chunk, (i + 1) * per_chunk, tile, loss, unroll=2)
        part = pl.ds(i * chunk, chunk)
        copy = pltpu.make_async_copy(out_ref.at[:, part], out_hbm.at[:, part], out_sem.at[i])
        copy.start()
        out_copies.append(copy)
    loss_ref[...] = jnp.broadcast_to(
        (jnp.sum(loss, axis=0, keepdims=True) + row_terms).reshape(1, 1, LANES), loss_ref.shape
    )
    for copy in out_copies:
        copy.wait()


def per_device(mentor_score_matrix, learner_score_matrix, align_dev, align_slot, align_weight):
    owners = lax.axis_size("vocab")
    shards = owners * lax.axis_size("dp")
    rows, teacher_width = mentor_score_matrix.shape
    width = learner_score_matrix.shape[1]
    tb_local, topk = align_dev.shape
    edges = tb_local * topk
    halves = rows // LANES
    block_rows = halves * BLK
    packet_rows = MOST * block_rows + TAIL_ROWS
    chunks = BLK * BLK // LANES
    weight = (
        align_weight.reshape(tb_local, topk, chunks, LANES)
        .transpose(0, 2, 1, 3)
        .reshape(tb_local * chunks * topk, LANES)
    )
    vmem = pl.BlockSpec(memory_space=pltpu.VMEM)
    hbm = pl.BlockSpec(memory_space=pl.ANY)
    outgoing = pl.pallas_call(
        send_kernel,
        out_shape=jax.ShapeDtypeStruct((owners, packet_rows, LANES), BF16),
        in_specs=[vmem, vmem, vmem, hbm, vmem],
        out_specs=hbm,
        scratch_shapes=[
            pltpu.VMEM((rows, width), BF16),
            pltpu.VMEM((teacher_width // LANES, rows, LANES), BF16),
            pltpu.VMEM((halves, LANES, LANES), F32),
            pltpu.VMEM((edges, block_rows, LANES), BF16),
            pltpu.VMEM((owners, TAIL_ROWS, LANES), BF16),
            pltpu.VMEM((8, LANES), F32),
            pltpu.VMEM((32, LANES), jnp.int32),
            pltpu.SMEM((32, LANES), jnp.int32),
            pltpu.SemaphoreType.DMA,
            pltpu.SemaphoreType.DMA,
            pltpu.SemaphoreType.DMA,
            pltpu.SemaphoreType.DMA,
        ],
        name="send",
    )(align_dev.T, align_slot.T, mentor_score_matrix, learner_score_matrix, weight)
    arrived = lax.all_to_all(outgoing, "vocab", split_axis=0, concat_axis=0, tiled=True)
    scaled_grad, loss = pl.pallas_call(
        receive_kernel,
        out_shape=(
            jax.ShapeDtypeStruct((rows, width), BF16),
            jax.ShapeDtypeStruct((shards, 1, LANES), F32),
        ),
        in_specs=[hbm, hbm],
        out_specs=(hbm, vmem),
        scratch_shapes=[
            pltpu.VMEM((rows, width), BF16),
            pltpu.VMEM((rows, width), BF16),
            pltpu.VMEM((owners, MOST * block_rows, LANES), BF16),
            pltpu.VMEM((owners, TAIL_ROWS, LANES), BF16),
            pltpu.VMEM((owners * TAIL_ROWS, LANES), F32),
            pltpu.VMEM((halves * owners, LANES), F32),
            pltpu.VMEM((owners, LANES), jnp.int32),
            pltpu.SMEM((owners, LANES), jnp.int32),
            pltpu.VMEM((halves * (width + BLK), LANES), F32),
            pltpu.VMEM((rows, LANES), F32),
            pltpu.SemaphoreType.DMA((8,)),
            pltpu.SemaphoreType.DMA,
            pltpu.SemaphoreType.DMA,
            pltpu.SemaphoreType.DMA,
            pltpu.SemaphoreType.DMA((8,)),
        ],
        name="receive",
    )(arrived, learner_score_matrix)
    parts = lax.all_to_all(loss, ("dp", "vocab"), split_axis=0, concat_axis=0, tiled=True)
    tokens = float(rows * lax.axis_size("dp"))
    unit = math.log(2.0) / (width * owners)
    divergence = SMOOTHING_HEAT * SMOOTHING_HEAT * unit / tokens * jnp.sum(parts)
    return scaled_grad, divergence


def solution(mesh):
    in_specs = (
        P("dp", "vocab"),
        P("dp", "vocab"),
        P("vocab", None),
        P("vocab", None),
        P("vocab", None, None),
    )
    out_specs = (P("dp", "vocab"), P())
    return jax.shard_map(
        per_device, mesh=mesh, in_specs=in_specs, out_specs=out_specs, check_vma=False
    )
```

```python
import math

import jax
import jax.numpy as jnp
from jax import lax
from jax.experimental import pallas as pl
from jax.experimental.pallas import tpu as pltpu
from jax.sharding import PartitionSpec as P

BLK = 64
LANES = 128
SMOOTHING_HEAT = 2
MOST = 2
TAIL_ROWS = 16
CODE_ROW = 7
EXP2_SCALE = math.log2(math.e) / SMOOTHING_HEAT
TINY = 2.0**-126

F32 = jnp.float32
BF16 = jnp.bfloat16


def split2(x):
    hi = x.astype(BF16).astype(F32)
    return hi, x - hi


def send_kernel(
    dev_ref, slot_ref, x_ref, y_hbm, w_ref, out_ref, y_ref, probs, high_v, term, tail, edge_v, pos_v,
    pos_s, sem, tail_sem, y_sem, pos_sem,
):
    rows, width = x_ref.shape
    owners = out_ref.shape[0]
    halves = rows // LANES
    pairs = width // LANES
    student_tiles = y_ref.shape[1] // LANES
    topk, blocks = dev_ref.shape
    block_rows = halves * BLK
    padded = pos_v.shape[0]

    y_copy = pltpu.make_async_copy(y_hbm, y_ref, y_sem)
    y_copy.start()

    edge_v[...] = jnp.full((8, LANES), -1.0, F32)
    edge_v[:topk, :blocks] = dev_ref[...].astype(F32)
    edge_v[topk : 2 * topk, :blocks] = slot_ref[...].astype(F32)
    edge_rows = edge_v[...]
    edge_cols = edge_rows.T[:padded]
    below = lax.broadcasted_iota(jnp.int32, (padded, LANES), 1) < lax.broadcasted_iota(
        jnp.int32, (padded, LANES), 0
    )
    edge_lane = lax.broadcasted_iota(jnp.int32, (padded, LANES), 1)
    code = jnp.zeros((padded, LANES), F32)
    places = jnp.zeros((padded, LANES), F32)
    for k in range(topk):
        owner = edge_cols[:, k : k + 1]
        hits = jnp.zeros((padded, LANES), F32)
        for other in range(topk):
            same = (owner == edge_rows[other : other + 1, :]) & below
            hits = hits + jnp.where(same, 1.0, 0.0)
        place = owner * MOST + jnp.sum(hits, axis=1, keepdims=True)
        code = code + jnp.where(
            place == edge_lane.astype(F32), edge_cols[:, topk + k : topk + k + 1] + 1.0, 0.0
        )
        places = jnp.where(edge_lane == k, place, places)
    codes = jnp.sum(code, axis=0, keepdims=True) - 1.0
    pos_v[...] = places.astype(jnp.int32)
    pos_copy = pltpu.make_async_copy(pos_v, pos_s, pos_sem)
    pos_copy.start()

    def shard_max(ref, h, tiles):
        lanes = slice(h * LANES, (h + 1) * LANES)
        m = ref[lanes, :LANES]
        for t in range(1, tiles):
            m = jnp.maximum(m, ref[lanes, t * LANES : (t + 1) * LANES])
        return jnp.max(m.astype(F32), axis=1, keepdims=True)

    teacher_high, teacher_sum = [], []
    for h in range(halves):
        lanes = slice(h * LANES, (h + 1) * LANES)
        high = shard_max(x_ref, h, pairs)
        high_b = jnp.broadcast_to(high, (LANES, LANES))
        total = jnp.zeros((LANES, LANES), F32)
        for q in range(pairs):
            e = jnp.exp2((x_ref[lanes, q * LANES : (q + 1) * LANES].astype(F32) - high_b) * EXP2_SCALE)
            total = total + e
            probs[q, lanes, :] = e.astype(BF16)
        teacher_high.append(high)
        teacher_sum.append(jnp.sum(total, axis=1, keepdims=True))

    y_copy.wait()
    student_high = [shard_max(y_ref, h, student_tiles) for h in range(halves)]

    pos_copy.wait()

    def send_edges(q):
        for index in range(q * 2 * topk, (q + 1) * 2 * topk):
            place = pos_s[index // topk, index % topk]
            at = pl.multiple_of((place % MOST) * block_rows, block_rows)
            pltpu.make_async_copy(
                term.at[index], out_ref.at[place // MOST, pl.ds(at, block_rows), :], sem
            ).start()

    for h in range(halves):
        high_v[h] = jnp.broadcast_to(student_high[h], (LANES, LANES))
    lane = lax.broadcasted_iota(jnp.int32, (BLK, LANES), 1)
    even = lane % 2 == 0
    first = lane < BLK
    mass = jnp.zeros((8, rows), F32)
    student_total = [jnp.zeros((LANES, LANES), F32) for _ in range(halves)]
    items = [(h, t) for h in range(halves) for t in range(student_tiles)]
    for q in range(pairs):
        w = w_ref[q * LANES : (q + 1) * LANES, :].astype(F32).T
        a0, a1 = w[:BLK], w[BLK:]
        l0 = jnp.where(even, a0, pltpu.roll(a1, 1, 1))
        l1 = jnp.where(even, pltpu.roll(a0, LANES - 1, 1), a1)
        lhs = jnp.concatenate(
            [
                jnp.where(first, l0, 0.0),
                jnp.where(first, l1, 0.0),
                jnp.where(first, 0.0, l0),
                jnp.where(first, 0.0, l1),
            ],
            axis=0,
        ).astype(BF16)
        u = lax.dot_general(
            lhs, probs[q], (((1,), (1,)), ((), ())), preferred_element_type=F32
        )
        for h, t in items[len(items) * q // pairs : len(items) * (q + 1) // pairs]:
            y = y_ref[h * LANES : (h + 1) * LANES, t * LANES : (t + 1) * LANES].astype(F32)
            student_total[h] = student_total[h] + jnp.exp2((y - high_v[h]) * EXP2_SCALE)
        mass = mass + jnp.sum(u.reshape(4 * BLK // 8, 8, rows), axis=0)
        u = u.astype(BF16)
        for edge in range(2 * topk):
            for h in range(halves):
                term[q * 2 * topk + edge, h * BLK : (h + 1) * BLK, :] = u[
                    edge * BLK : (edge + 1) * BLK, h * LANES : (h + 1) * LANES
                ]
        if q > 0:
            send_edges(q - 1)
    send_edges(pairs - 1)

    row_lane = lax.broadcasted_iota(jnp.int32, (LANES, LANES), 1)
    r_hi, r_lo = split2(jnp.sum(mass, axis=0, keepdims=True))
    sub = lax.broadcasted_iota(jnp.int32, (8, LANES), 0)
    pieces = []
    for h in range(halves):
        t_hi, t_lo = split2(teacher_sum[h])
        student_sum = jnp.sum(student_total[h], axis=1, keepdims=True)
        s_hi, s_lo = split2(student_high[h] * EXP2_SCALE + jnp.log2(student_sum))
        columns = jnp.zeros((LANES, LANES), F32)
        for i, v in ((0, teacher_high[h]), (1, t_hi), (2, t_lo), (5, s_hi), (6, s_lo)):
            columns = jnp.where(row_lane == i, v, columns)
        lanes = slice(h * LANES, (h + 1) * LANES)
        s = columns.T[:8]
        s = jnp.where(sub == 3, r_hi[:, lanes], s)
        s = jnp.where(sub == 4, r_lo[:, lanes], s)
        pieces.append(jnp.where(sub == CODE_ROW, codes, s))
    stats = jnp.concatenate(pieces, axis=0).astype(BF16)
    for i in range(owners):
        tail[i] = stats
    tail_copy = pltpu.make_async_copy(
        tail, out_ref.at[:, pl.ds(MOST * block_rows, TAIL_ROWS), :], tail_sem
    )
    tail_copy.start()
    pltpu.make_async_copy(term, term, sem).wait()
    tail_copy.wait()


def receive_kernel(
    arr_ref, y_hbm, out_hbm, loss_ref, y_ref, out_ref, buf, tail, wide, scale, code_v, code_s, acc,
    bias, sem, tail_sem, code_sem, y_sem, out_sem,
):
    owners = arr_ref.shape[0]
    width, rows = y_ref.shape
    halves = rows // LANES
    tiles = width // LANES
    block_rows = halves * BLK
    groups = sem.shape[0]
    per = owners // groups
    span = width + BLK
    vocab_width = float(width * owners)
    me = lax.axis_index("vocab")

    tail_copy = pltpu.make_async_copy(
        arr_ref.at[:, pl.ds(MOST * block_rows, TAIL_ROWS), :], tail, tail_sem
    )
    tail_copy.start()

    def block_copy(g):
        return pltpu.make_async_copy(
            arr_ref.at[pl.ds(g * per, per), pl.ds(0, MOST * block_rows), :],
            buf.at[pl.ds(g * per, per)],
            sem.at[g],
        )

    for g in range(groups):
        block_copy(g).start()
    y_copy = pltpu.make_async_copy(y_hbm, y_ref, y_sem)
    y_copy.start()

    for h in range(halves):

        @pl.loop(0, width // 512)
        def _(i):
            acc[pl.ds(pl.multiple_of(h * span + i * 512, BLK), 512), :] = jnp.full((512, LANES), TINY, F32)

    tail_copy.wait()
    wide[...] = tail[...].astype(F32).reshape(owners * TAIL_ROWS, LANES)
    codes = wide[pl.ds(CODE_ROW, owners, stride=TAIL_ROWS), :].astype(jnp.int32)
    code_v[...] = jnp.where(codes < 0, width // BLK, codes)
    code_copy = pltpu.make_async_copy(code_v, code_s, code_sem)
    code_copy.start()

    row_terms = jnp.zeros((1, LANES), F32)
    for h in range(halves):

        def stat(i):
            return wide[pl.ds(8 * h + i, owners, stride=TAIL_ROWS), :]

        t_high = stat(0)
        t_top = jnp.max(t_high, axis=0, keepdims=True)
        t_rel = jnp.exp2((t_high - t_top) * EXP2_SCALE)
        inv = vocab_width / jnp.sum(t_rel * (stat(1) + stat(2)), axis=0, keepdims=True)
        scale_h = t_rel * inv
        scale[h * owners : (h + 1) * owners, :] = scale_h
        total = jnp.sum(scale_h * (stat(3) + stat(4)), axis=0, keepdims=True)
        log_total = jnp.log2(total)
        s_lse = stat(5) + stat(6)
        s_top = jnp.max(s_lse, axis=0, keepdims=True)
        lse = s_top + jnp.log2(jnp.sum(jnp.exp2(s_lse - s_top), axis=0, keepdims=True))
        bias[h : h + 1, :] = lse - log_total
        row_terms = row_terms + total * (log_total - math.log2(vocab_width)) * (1.0 / owners)

    code_copy.wait()
    for g in range(groups):
        block_copy(g).wait()

        def add_source(i, carry):
            src = g * per + i
            for slot in range(MOST):
                c = code_s[src, me * MOST + slot]
                for h in range(halves):
                    at = pl.ds(pl.multiple_of(h * span + c * BLK, BLK), BLK)
                    lo = slot * block_rows + h * BLK
                    term = buf[src, lo : lo + BLK, :].astype(F32)
                    acc[at, :] = acc[at, :] + term * scale[pl.ds(h * owners + src, 1), :]
            return carry

        lax.fori_loop(0, per, add_source, 0, unroll=2)

    y_copy.wait()
    chunks = out_sem.shape[0]
    chunk = width // chunks

    def tile(t, loss):
        cols = pl.ds(pl.multiple_of(t * LANES, LANES), LANES)
        for h in range(halves):
            lanes = slice(h * LANES, (h + 1) * LANES)
            target = acc[pl.ds(pl.multiple_of(h * span + t * LANES, BLK), LANES), :]
            goal = y_ref[cols, lanes].astype(F32) * EXP2_SCALE - bias[h : h + 1, :]
            out_ref[lanes, cols] = (jnp.exp2(goal) - target).astype(BF16).T
            term = target * (jnp.log2(target) - goal)
            loss = loss + jnp.sum(term.reshape(LANES // 32, 32, LANES), axis=0)
        return loss

    loss = jnp.zeros((32, LANES), F32)
    out_copies = []
    for i in range(chunks):
        per_chunk = tiles // chunks
        loss = lax.fori_loop(i * per_chunk, (i + 1) * per_chunk, tile, loss, unroll=True)
        part = pl.ds(i * chunk, chunk)
        copy = pltpu.make_async_copy(out_ref.at[:, part], out_hbm.at[:, part], out_sem.at[i])
        copy.start()
        out_copies.append(copy)
    loss_ref[...] = jnp.broadcast_to(
        (jnp.sum(loss, axis=0, keepdims=True) + row_terms).reshape(1, 1, LANES), loss_ref.shape
    )
    for copy in out_copies:
        copy.wait()


def per_device(mentor_score_matrix, learner_score_matrix, align_dev, align_slot, align_weight):
    owners = lax.axis_size("vocab")
    shards = owners * lax.axis_size("dp")
    rows, teacher_width = mentor_score_matrix.shape
    width = learner_score_matrix.shape[1]
    tb_local, topk = align_dev.shape
    edges = tb_local * topk
    halves = rows // LANES
    block_rows = halves * BLK
    packet_rows = MOST * block_rows + TAIL_ROWS
    chunks = BLK * BLK // LANES
    weight = (
        align_weight.reshape(tb_local, topk, chunks, LANES)
        .transpose(0, 2, 1, 3)
        .reshape(tb_local * chunks * topk, LANES)
    )
    vmem = pl.BlockSpec(memory_space=pltpu.VMEM)
    hbm = pl.BlockSpec(memory_space=pl.ANY)
    outgoing = pl.pallas_call(
        send_kernel,
        out_shape=jax.ShapeDtypeStruct((owners, packet_rows, LANES), BF16),
        in_specs=[vmem, vmem, vmem, hbm, vmem],
        out_specs=hbm,
        scratch_shapes=[
            pltpu.VMEM((rows, width), BF16),
            pltpu.VMEM((teacher_width // LANES, rows, LANES), BF16),
            pltpu.VMEM((halves, LANES, LANES), F32),
            pltpu.VMEM((edges, block_rows, LANES), BF16),
            pltpu.VMEM((owners, TAIL_ROWS, LANES), BF16),
            pltpu.VMEM((8, LANES), F32),
            pltpu.VMEM((32, LANES), jnp.int32),
            pltpu.SMEM((32, LANES), jnp.int32),
            pltpu.SemaphoreType.DMA,
            pltpu.SemaphoreType.DMA,
            pltpu.SemaphoreType.DMA,
            pltpu.SemaphoreType.DMA,
        ],
        name="send",
    )(align_dev.T, align_slot.T, mentor_score_matrix, learner_score_matrix, weight)
    arrived = lax.all_to_all(outgoing, "vocab", split_axis=0, concat_axis=0, tiled=True)
    scaled_grad, loss = pl.pallas_call(
        receive_kernel,
        out_shape=(
            jax.ShapeDtypeStruct((rows, width), BF16),
            jax.ShapeDtypeStruct((shards, 1, LANES), F32),
        ),
        in_specs=[hbm, hbm],
        out_specs=(hbm, vmem),
        scratch_shapes=[
            pltpu.VMEM((width, rows), BF16),
            pltpu.VMEM((rows, width), BF16),
            pltpu.VMEM((owners, MOST * block_rows, LANES), BF16),
            pltpu.VMEM((owners, TAIL_ROWS, LANES), BF16),
            pltpu.VMEM((owners * TAIL_ROWS, LANES), F32),
            pltpu.VMEM((halves * owners, LANES), F32),
            pltpu.VMEM((owners, LANES), jnp.int32),
            pltpu.SMEM((owners, LANES), jnp.int32),
            pltpu.VMEM((halves * (width + BLK), LANES), F32),
            pltpu.VMEM((8, LANES), F32),
            pltpu.SemaphoreType.DMA((8,)),
            pltpu.SemaphoreType.DMA,
            pltpu.SemaphoreType.DMA,
            pltpu.SemaphoreType.DMA,
            pltpu.SemaphoreType.DMA((8,)),
        ],
        name="receive",
    )(arrived, learner_score_matrix.T)
    parts = lax.all_to_all(loss, ("dp", "vocab"), split_axis=0, concat_axis=0, tiled=True)
    tokens = float(rows * lax.axis_size("dp"))
    unit = math.log(2.0) / (width * owners)
    divergence = SMOOTHING_HEAT * SMOOTHING_HEAT * unit / tokens * jnp.sum(parts)
    return scaled_grad, divergence


def solution(mesh):
    in_specs = (
        P("dp", "vocab"),
        P("dp", "vocab"),
        P("vocab", None),
        P("vocab", None),
        P("vocab", None, None),
    )
    out_specs = (P("dp", "vocab"), P())
    return jax.shard_map(
        per_device, mesh=mesh, in_specs=in_specs, out_specs=out_specs, check_vma=False
    )
```

```python
import math

import jax
import jax.numpy as jnp
from jax import lax
from jax.experimental import pallas as pl
from jax.experimental.pallas import tpu as pltpu
from jax.sharding import PartitionSpec as P

BLK = 64
LANES = 128
SMOOTHING_HEAT = 2
MOST = 2
TAIL_ROWS = 16
CODE_ROW = 7
EXP2_SCALE = math.log2(math.e) / SMOOTHING_HEAT
TINY = 2.0**-126

F32 = jnp.float32
BF16 = jnp.bfloat16


def split2(x):
    hi = x.astype(BF16).astype(F32)
    return hi, x - hi


def send_kernel(
    dev_ref, slot_ref, x_hbm, y_hbm, w_hbm, out_ref, yt_hbm, x_ref, w_ref, y_ref, yt_ref, probs, high_v, term, tail, edge_v, pos_v,
    pos_s, sem, tail_sem, y_sem, yt_sem, pos_sem, x_sem, w_sem,
):
    rows, width = x_ref.shape
    owners = out_ref.shape[0]
    halves = rows // LANES
    pairs = width // LANES
    student_tiles = y_ref.shape[1] // LANES
    topk, blocks = dev_ref.shape
    block_rows = halves * BLK
    padded = pos_v.shape[0]

    def x_copy(h):
        lanes = pl.ds(h * LANES, LANES)
        return pltpu.make_async_copy(x_hbm.at[lanes], x_ref.at[lanes], x_sem.at[h])

    for h in range(halves):
        x_copy(h).start()
    y_copy = pltpu.make_async_copy(y_hbm, y_ref, y_sem)
    y_copy.start()
    w_copy = pltpu.make_async_copy(w_hbm, w_ref, w_sem)
    w_copy.start()

    edge_v[...] = jnp.full((8, LANES), -1.0, F32)
    edge_v[:topk, :blocks] = dev_ref[...].astype(F32)
    edge_v[topk : 2 * topk, :blocks] = slot_ref[...].astype(F32)
    edge_rows = edge_v[...]
    edge_cols = edge_rows.T[:padded]
    below = lax.broadcasted_iota(jnp.int32, (padded, LANES), 1) < lax.broadcasted_iota(
        jnp.int32, (padded, LANES), 0
    )
    edge_lane = lax.broadcasted_iota(jnp.int32, (padded, LANES), 1)
    code = jnp.zeros((padded, LANES), F32)
    places = jnp.zeros((padded, LANES), F32)
    for k in range(topk):
        owner = edge_cols[:, k : k + 1]
        hits = jnp.zeros((padded, LANES), F32)
        for other in range(topk):
            same = (owner == edge_rows[other : other + 1, :]) & below
            hits = hits + jnp.where(same, 1.0, 0.0)
        place = owner * MOST + jnp.sum(hits, axis=1, keepdims=True)
        code = code + jnp.where(
            place == edge_lane.astype(F32), edge_cols[:, topk + k : topk + k + 1] + 1.0, 0.0
        )
        places = jnp.where(edge_lane == k, place, places)
    codes = jnp.sum(code, axis=0, keepdims=True) - 1.0
    pos_v[...] = places.astype(jnp.int32)
    pos_copy = pltpu.make_async_copy(pos_v, pos_s, pos_sem)
    pos_copy.start()

    def shard_max(ref, h, tiles):
        lanes = slice(h * LANES, (h + 1) * LANES)
        m = ref[lanes, :LANES]
        for t in range(1, tiles):
            m = jnp.maximum(m, ref[lanes, t * LANES : (t + 1) * LANES])
        return jnp.max(m.astype(F32), axis=1, keepdims=True)

    for h in range(halves):
        x_copy(h).wait()
    teacher_high, teacher_sum = [], []
    for h in range(halves):
        lanes = slice(h * LANES, (h + 1) * LANES)
        high = shard_max(x_ref, h, pairs)
        high_b = jnp.broadcast_to(high, (LANES, LANES))
        total = jnp.zeros((LANES, LANES), F32)
        for q in range(pairs):
            e = jnp.exp2((x_ref[lanes, q * LANES : (q + 1) * LANES].astype(F32) - high_b) * EXP2_SCALE)
            total = total + e
            probs[q, lanes, :] = e.astype(BF16)
        teacher_high.append(high)
        teacher_sum.append(jnp.sum(total, axis=1, keepdims=True))

    y_copy.wait()
    w_copy.wait()
    student_high = [shard_max(y_ref, h, student_tiles) for h in range(halves)]

    pos_copy.wait()

    def send_edges(q):
        for index in range(q * 2 * topk, (q + 1) * 2 * topk):
            place = pos_s[index // topk, index % topk]
            at = pl.multiple_of((place % MOST) * block_rows, block_rows)
            pltpu.make_async_copy(
                term.at[index], out_ref.at[place // MOST, pl.ds(at, block_rows), :], sem
            ).start()

    for h in range(halves):
        high_v[h] = jnp.broadcast_to(student_high[h], (LANES, LANES))
    lane = lax.broadcasted_iota(jnp.int32, (BLK, LANES), 1)
    even = lane % 2 == 0
    first = lane < BLK
    mass = jnp.zeros((8, rows), F32)
    student_total = [jnp.zeros((LANES, LANES), F32) for _ in range(halves)]
    items = [(h, t) for h in range(halves) for t in range(student_tiles)]
    yt_parts = yt_sem.shape[1]
    yt_rows = student_tiles * LANES // yt_parts

    def yt_copy(h, i):
        part = pl.ds(i * yt_rows, yt_rows)
        return pltpu.make_async_copy(yt_ref.at[h, part], yt_hbm.at[h, part], yt_sem.at[h, i])

    for q in range(pairs):
        w = w_ref[q * LANES : (q + 1) * LANES, :].astype(F32).T
        a0, a1 = w[:BLK], w[BLK:]
        l0 = jnp.where(even, a0, pltpu.roll(a1, 1, 1))
        l1 = jnp.where(even, pltpu.roll(a0, LANES - 1, 1), a1)
        lhs = jnp.concatenate(
            [
                jnp.where(first, l0, 0.0),
                jnp.where(first, l1, 0.0),
                jnp.where(first, 0.0, l0),
                jnp.where(first, 0.0, l1),
            ],
            axis=0,
        ).astype(BF16)
        u = lax.dot_general(
            lhs, probs[q], (((1,), (1,)), ((), ())), preferred_element_type=F32
        )
        for h, t in items[len(items) * q // pairs : len(items) * (q + 1) // pairs]:
            y = y_ref[h * LANES : (h + 1) * LANES, t * LANES : (t + 1) * LANES].astype(F32)
            student_total[h] = student_total[h] + jnp.exp2((y - high_v[h]) * EXP2_SCALE)
            yt_ref[h, t * LANES : (t + 1) * LANES, :] = y_ref[
                h * LANES : (h + 1) * LANES, t * LANES : (t + 1) * LANES
            ].T
            if (t + 1) * LANES % yt_rows == 0:
                yt_copy(h, (t + 1) * LANES // yt_rows - 1).start()
        mass = mass + jnp.sum(u.reshape(4 * BLK // 8, 8, rows), axis=0)
        u = u.astype(BF16)
        for edge in range(2 * topk):
            for h in range(halves):
                term[q * 2 * topk + edge, h * BLK : (h + 1) * BLK, :] = u[
                    edge * BLK : (edge + 1) * BLK, h * LANES : (h + 1) * LANES
                ]
        if q > 0:
            send_edges(q - 1)
    send_edges(pairs - 1)

    row_lane = lax.broadcasted_iota(jnp.int32, (LANES, LANES), 1)
    r_hi, r_lo = split2(jnp.sum(mass, axis=0, keepdims=True))
    sub = lax.broadcasted_iota(jnp.int32, (8, LANES), 0)
    pieces = []
    for h in range(halves):
        t_hi, t_lo = split2(teacher_sum[h])
        student_sum = jnp.sum(student_total[h], axis=1, keepdims=True)
        s_hi, s_lo = split2(student_high[h] * EXP2_SCALE + jnp.log2(student_sum))
        columns = jnp.zeros((LANES, LANES), F32)
        for i, v in ((0, teacher_high[h]), (1, t_hi), (2, t_lo), (5, s_hi), (6, s_lo)):
            columns = jnp.where(row_lane == i, v, columns)
        lanes = slice(h * LANES, (h + 1) * LANES)
        s = columns.T[:8]
        s = jnp.where(sub == 3, r_hi[:, lanes], s)
        s = jnp.where(sub == 4, r_lo[:, lanes], s)
        pieces.append(jnp.where(sub == CODE_ROW, codes, s))
    stats = jnp.concatenate(pieces, axis=0).astype(BF16)
    for i in range(owners):
        tail[i] = stats
    tail_copy = pltpu.make_async_copy(
        tail, out_ref.at[:, pl.ds(MOST * block_rows, TAIL_ROWS), :], tail_sem
    )
    tail_copy.start()
    pltpu.make_async_copy(term, term, sem).wait()
    tail_copy.wait()
    for h in range(halves):
        for i in range(yt_parts):
            yt_copy(h, i).wait()


def receive_kernel(
    arr_ref, y_hbm, out_hbm, loss_ref, y_ref, out_ref, buf, tail, wide, scale, code_v, code_s, acc,
    bias, sem, tail_sem, code_sem, y_sem, out_sem,
):
    owners = arr_ref.shape[0]
    halves, width, _ = y_ref.shape
    tiles = width // LANES
    block_rows = halves * BLK
    groups = sem.shape[0]
    per = owners // groups
    span = width + BLK
    vocab_width = float(width * owners)
    me = lax.axis_index("vocab")

    tail_copy = pltpu.make_async_copy(
        arr_ref.at[:, pl.ds(MOST * block_rows, TAIL_ROWS), :], tail, tail_sem
    )
    tail_copy.start()

    def block_copy(g):
        return pltpu.make_async_copy(
            arr_ref.at[pl.ds(g * per, per), pl.ds(0, MOST * block_rows), :],
            buf.at[pl.ds(g * per, per)],
            sem.at[g],
        )

    for g in range(groups):
        block_copy(g).start()
    y_copy = pltpu.make_async_copy(y_hbm, y_ref, y_sem)
    y_copy.start()

    for h in range(halves):

        @pl.loop(0, width // 512)
        def _(i):
            acc[pl.ds(pl.multiple_of(h * span + i * 512, BLK), 512), :] = jnp.full((512, LANES), TINY, F32)

    tail_copy.wait()
    wide[...] = tail[...].astype(F32).reshape(owners * TAIL_ROWS, LANES)
    codes = wide[pl.ds(CODE_ROW, owners, stride=TAIL_ROWS), :].astype(jnp.int32)
    code_v[...] = jnp.where(codes < 0, width // BLK, codes)
    code_copy = pltpu.make_async_copy(code_v, code_s, code_sem)
    code_copy.start()

    row_terms = jnp.zeros((1, LANES), F32)
    for h in range(halves):

        def stat(i):
            return wide[pl.ds(8 * h + i, owners, stride=TAIL_ROWS), :]

        t_high = stat(0)
        t_top = jnp.max(t_high, axis=0, keepdims=True)
        t_rel = jnp.exp2((t_high - t_top) * EXP2_SCALE)
        inv = vocab_width / jnp.sum(t_rel * (stat(1) + stat(2)), axis=0, keepdims=True)
        scale_h = t_rel * inv
        scale[h * owners : (h + 1) * owners, :] = scale_h
        total = jnp.sum(scale_h * (stat(3) + stat(4)), axis=0, keepdims=True)
        log_total = jnp.log2(total)
        s_lse = stat(5) + stat(6)
        s_top = jnp.max(s_lse, axis=0, keepdims=True)
        lse = s_top + jnp.log2(jnp.sum(jnp.exp2(s_lse - s_top), axis=0, keepdims=True))
        bias[h : h + 1, :] = lse - log_total
        row_terms = row_terms + total * (log_total - math.log2(vocab_width)) * (1.0 / owners)

    code_copy.wait()
    for g in range(groups):
        block_copy(g).wait()

        def add_source(i, carry):
            src = g * per + i
            for slot in range(MOST):
                c = code_s[src, me * MOST + slot]
                for h in range(halves):
                    at = pl.ds(pl.multiple_of(h * span + c * BLK, BLK), BLK)
                    lo = slot * block_rows + h * BLK
                    term = buf[src, lo : lo + BLK, :].astype(F32)
                    acc[at, :] = acc[at, :] + term * scale[pl.ds(h * owners + src, 1), :]
            return carry

        lax.fori_loop(0, per, add_source, 0, unroll=2)

    y_copy.wait()
    chunks = out_sem.shape[0]
    chunk = width // chunks

    def tile(t, loss):
        cols = pl.ds(pl.multiple_of(t * LANES, LANES), LANES)
        for h in range(halves):
            lanes = slice(h * LANES, (h + 1) * LANES)
            target = acc[pl.ds(pl.multiple_of(h * span + t * LANES, BLK), LANES), :]
            goal = y_ref[h, cols, :].astype(F32) * EXP2_SCALE - bias[h : h + 1, :]
            out_ref[lanes, cols] = (jnp.exp2(goal) - target).astype(BF16).T
            term = target * (jnp.log2(target) - goal)
            loss = loss + jnp.sum(term.reshape(LANES // 32, 32, LANES), axis=0)
        return loss

    loss = jnp.zeros((32, LANES), F32)
    out_copies = []
    for i in range(chunks):
        per_chunk = tiles // chunks
        loss = lax.fori_loop(i * per_chunk, (i + 1) * per_chunk, tile, loss, unroll=True)
        part = pl.ds(i * chunk, chunk)
        copy = pltpu.make_async_copy(out_ref.at[:, part], out_hbm.at[:, part], out_sem.at[i])
        copy.start()
        out_copies.append(copy)
    loss_ref[...] = jnp.broadcast_to(
        (jnp.sum(loss, axis=0, keepdims=True) + row_terms).reshape(1, 1, LANES), loss_ref.shape
    )
    for copy in out_copies:
        copy.wait()


def per_device(mentor_score_matrix, learner_score_matrix, align_dev, align_slot, align_weight):
    owners = lax.axis_size("vocab")
    shards = owners * lax.axis_size("dp")
    rows, teacher_width = mentor_score_matrix.shape
    width = learner_score_matrix.shape[1]
    tb_local, topk = align_dev.shape
    edges = tb_local * topk
    halves = rows // LANES
    block_rows = halves * BLK
    packet_rows = MOST * block_rows + TAIL_ROWS
    chunks = BLK * BLK // LANES
    weight = (
        align_weight.reshape(tb_local, topk, chunks, LANES)
        .transpose(0, 2, 1, 3)
        .reshape(tb_local * chunks * topk, LANES)
    )
    vmem = pl.BlockSpec(memory_space=pltpu.VMEM)
    hbm = pl.BlockSpec(memory_space=pl.ANY)
    outgoing, learner_t = pl.pallas_call(
        send_kernel,
        out_shape=(
            jax.ShapeDtypeStruct((owners, packet_rows, LANES), BF16),
            jax.ShapeDtypeStruct((halves, width, LANES), BF16),
        ),
        in_specs=[vmem, vmem, hbm, hbm, hbm],
        out_specs=(hbm, hbm),
        scratch_shapes=[
            pltpu.VMEM((rows, teacher_width), BF16),
            pltpu.VMEM(weight.shape, BF16),
            pltpu.VMEM((rows, width), BF16),
            pltpu.VMEM((halves, width, LANES), BF16),
            pltpu.VMEM((teacher_width // LANES, rows, LANES), BF16),
            pltpu.VMEM((halves, LANES, LANES), F32),
            pltpu.VMEM((edges, block_rows, LANES), BF16),
            pltpu.VMEM((owners, TAIL_ROWS, LANES), BF16),
            pltpu.VMEM((8, LANES), F32),
            pltpu.VMEM((32, LANES), jnp.int32),
            pltpu.SMEM((32, LANES), jnp.int32),
            pltpu.SemaphoreType.DMA,
            pltpu.SemaphoreType.DMA,
            pltpu.SemaphoreType.DMA,
            pltpu.SemaphoreType.DMA((halves, 4)),
            pltpu.SemaphoreType.DMA,
            pltpu.SemaphoreType.DMA((halves,)),
            pltpu.SemaphoreType.DMA,
        ],
        name="send",
    )(align_dev.T, align_slot.T, mentor_score_matrix, learner_score_matrix, weight)
    arrived = lax.all_to_all(outgoing, "vocab", split_axis=0, concat_axis=0, tiled=True)
    scaled_grad, loss = pl.pallas_call(
        receive_kernel,
        out_shape=(
            jax.ShapeDtypeStruct((rows, width), BF16),
            jax.ShapeDtypeStruct((shards, 1, LANES), F32),
        ),
        in_specs=[hbm, hbm],
        out_specs=(hbm, vmem),
        scratch_shapes=[
            pltpu.VMEM((halves, width, LANES), BF16),
            pltpu.VMEM((rows, width), BF16),
            pltpu.VMEM((owners, MOST * block_rows, LANES), BF16),
            pltpu.VMEM((owners, TAIL_ROWS, LANES), BF16),
            pltpu.VMEM((owners * TAIL_ROWS, LANES), F32),
            pltpu.VMEM((halves * owners, LANES), F32),
            pltpu.VMEM((owners, LANES), jnp.int32),
            pltpu.SMEM((owners, LANES), jnp.int32),
            pltpu.VMEM((halves * (width + BLK), LANES), F32),
            pltpu.VMEM((8, LANES), F32),
            pltpu.SemaphoreType.DMA((8,)),
            pltpu.SemaphoreType.DMA,
            pltpu.SemaphoreType.DMA,
            pltpu.SemaphoreType.DMA,
            pltpu.SemaphoreType.DMA((8,)),
        ],
        name="receive",
    )(arrived, learner_t)
    parts = lax.all_to_all(loss, ("dp", "vocab"), split_axis=0, concat_axis=0, tiled=True)
    tokens = float(rows * lax.axis_size("dp"))
    unit = math.log(2.0) / (width * owners)
    divergence = SMOOTHING_HEAT * SMOOTHING_HEAT * unit / tokens * jnp.sum(parts)
    return scaled_grad, divergence


def solution(mesh):
    in_specs = (
        P("dp", "vocab"),
        P("dp", "vocab"),
        P("vocab", None),
        P("vocab", None),
        P("vocab", None, None),
    )
    out_specs = (P("dp", "vocab"), P())
    return jax.shard_map(
        per_device, mesh=mesh, in_specs=in_specs, out_specs=out_specs, check_vma=False
    )
```

```python
import math

import jax
import jax.numpy as jnp
from jax import lax
from jax.experimental import pallas as pl
from jax.experimental.pallas import tpu as pltpu
from jax.sharding import PartitionSpec as P

BLK = 64
LANES = 128
SMOOTHING_HEAT = 2
MOST = 2
TAIL_ROWS = 16
CODE_ROW = 7
EXP2_SCALE = math.log2(math.e) / SMOOTHING_HEAT
TINY = 2.0**-126

F32 = jnp.float32
BF16 = jnp.bfloat16


def split2(x):
    hi = x.astype(BF16).astype(F32)
    return hi, x - hi


def send_kernel(
    dev_hbm, slot_hbm, x_hbm, y_hbm, w_hbm, out_ref, yt_ref, dev_ref, slot_ref, x_ref, w_ref, y_ref,
    probs, high_v, edge_v, pos_v, pos_s, dev_sem, slot_sem, y_sem, pos_sem, x_sem, w_sem,
):
    rows, width = x_ref.shape
    owners = out_ref.shape[0]
    halves = rows // LANES
    pairs = width // LANES
    student_tiles = y_ref.shape[1] // LANES
    topk, blocks = dev_ref.shape
    block_rows = halves * BLK
    padded = pos_v.shape[0]

    def x_copy(h):
        lanes = pl.ds(h * LANES, LANES)
        return pltpu.make_async_copy(x_hbm.at[lanes], x_ref.at[lanes], x_sem.at[h])

    dev_copy = pltpu.make_async_copy(dev_hbm, dev_ref, dev_sem)
    dev_copy.start()
    slot_copy = pltpu.make_async_copy(slot_hbm, slot_ref, slot_sem)
    slot_copy.start()
    for h in range(halves):
        x_copy(h).start()
    y_copy = pltpu.make_async_copy(y_hbm, y_ref, y_sem)
    y_copy.start()
    w_copy = pltpu.make_async_copy(w_hbm, w_ref, w_sem)
    w_copy.start()

    edge_v[...] = jnp.full((8, LANES), -1.0, F32)
    dev_copy.wait()
    slot_copy.wait()
    edge_v[:topk, :blocks] = dev_ref[...].astype(F32)
    edge_v[topk : 2 * topk, :blocks] = slot_ref[...].astype(F32)
    edge_rows = edge_v[...]
    edge_cols = edge_rows.T[:padded]
    below = lax.broadcasted_iota(jnp.int32, (padded, LANES), 1) < lax.broadcasted_iota(
        jnp.int32, (padded, LANES), 0
    )
    edge_lane = lax.broadcasted_iota(jnp.int32, (padded, LANES), 1)
    code = jnp.zeros((padded, LANES), F32)
    places = jnp.zeros((padded, LANES), F32)
    for k in range(topk):
        owner = edge_cols[:, k : k + 1]
        hits = jnp.zeros((padded, LANES), F32)
        for other in range(topk):
            same = (owner == edge_rows[other : other + 1, :]) & below
            hits = hits + jnp.where(same, 1.0, 0.0)
        place = owner * MOST + jnp.sum(hits, axis=1, keepdims=True)
        code = code + jnp.where(
            place == edge_lane.astype(F32), edge_cols[:, topk + k : topk + k + 1] + 1.0, 0.0
        )
        places = jnp.where(edge_lane == k, place, places)
    codes = jnp.sum(code, axis=0, keepdims=True) - 1.0
    pos_v[...] = places.astype(jnp.int32)
    pos_copy = pltpu.make_async_copy(pos_v, pos_s, pos_sem)
    pos_copy.start()

    def shard_max(ref, h, tiles):
        lanes = slice(h * LANES, (h + 1) * LANES)
        m = ref[lanes, :LANES]
        for t in range(1, tiles):
            m = jnp.maximum(m, ref[lanes, t * LANES : (t + 1) * LANES])
        return jnp.max(m.astype(F32), axis=1, keepdims=True)

    for h in range(halves):
        x_copy(h).wait()
    teacher_high, teacher_sum = [], []
    for h in range(halves):
        lanes = slice(h * LANES, (h + 1) * LANES)
        high = shard_max(x_ref, h, pairs)
        high_b = jnp.broadcast_to(high, (LANES, LANES))
        total = jnp.zeros((LANES, LANES), F32)
        for q in range(pairs):
            e = jnp.exp2((x_ref[lanes, q * LANES : (q + 1) * LANES].astype(F32) - high_b) * EXP2_SCALE)
            total = total + e
            probs[q, lanes, :] = e.astype(BF16)
        teacher_high.append(high)
        teacher_sum.append(jnp.sum(total, axis=1, keepdims=True))

    y_copy.wait()
    w_copy.wait()
    student_high = [shard_max(y_ref, h, student_tiles) for h in range(halves)]

    pos_copy.wait()

    for h in range(halves):
        high_v[h] = jnp.broadcast_to(student_high[h], (LANES, LANES))
    lane = lax.broadcasted_iota(jnp.int32, (BLK, LANES), 1)
    even = lane % 2 == 0
    first = lane < BLK
    mass = jnp.zeros((8, rows), F32)
    student_total = [jnp.zeros((LANES, LANES), F32) for _ in range(halves)]
    items = [(h, t) for h in range(halves) for t in range(student_tiles)]
    for q in range(pairs):
        w = w_ref[q * LANES : (q + 1) * LANES, :].astype(F32).T
        a0, a1 = w[:BLK], w[BLK:]
        l0 = jnp.where(even, a0, pltpu.roll(a1, 1, 1))
        l1 = jnp.where(even, pltpu.roll(a0, LANES - 1, 1), a1)
        lhs = jnp.concatenate(
            [
                jnp.where(first, l0, 0.0),
                jnp.where(first, l1, 0.0),
                jnp.where(first, 0.0, l0),
                jnp.where(first, 0.0, l1),
            ],
            axis=0,
        ).astype(BF16)
        u = lax.dot_general(
            lhs, probs[q], (((1,), (1,)), ((), ())), preferred_element_type=F32
        )
        for h, t in items[len(items) * q // pairs : len(items) * (q + 1) // pairs]:
            y = y_ref[h * LANES : (h + 1) * LANES, t * LANES : (t + 1) * LANES].astype(F32)
            student_total[h] = student_total[h] + jnp.exp2((y - high_v[h]) * EXP2_SCALE)
            yt_ref[h, t * LANES : (t + 1) * LANES, :] = y_ref[
                h * LANES : (h + 1) * LANES, t * LANES : (t + 1) * LANES
            ].T
        mass = mass + jnp.sum(u.reshape(4 * BLK // 8, 8, rows), axis=0)
        u = u.astype(BF16)
        for edge in range(2 * topk):
            place = pos_s[2 * q + edge // topk, edge % topk]
            at = pl.multiple_of((place % MOST) * block_rows, block_rows)
            for h in range(halves):
                out_ref[place // MOST, pl.ds(at + h * BLK, BLK), :] = u[
                    edge * BLK : (edge + 1) * BLK, h * LANES : (h + 1) * LANES
                ]

    row_lane = lax.broadcasted_iota(jnp.int32, (LANES, LANES), 1)
    r_hi, r_lo = split2(jnp.sum(mass, axis=0, keepdims=True))
    sub = lax.broadcasted_iota(jnp.int32, (8, LANES), 0)
    pieces = []
    for h in range(halves):
        t_hi, t_lo = split2(teacher_sum[h])
        student_sum = jnp.sum(student_total[h], axis=1, keepdims=True)
        s_hi, s_lo = split2(student_high[h] * EXP2_SCALE + jnp.log2(student_sum))
        columns = jnp.zeros((LANES, LANES), F32)
        for i, v in ((0, teacher_high[h]), (1, t_hi), (2, t_lo), (5, s_hi), (6, s_lo)):
            columns = jnp.where(row_lane == i, v, columns)
        lanes = slice(h * LANES, (h + 1) * LANES)
        s = columns.T[:8]
        s = jnp.where(sub == 3, r_hi[:, lanes], s)
        s = jnp.where(sub == 4, r_lo[:, lanes], s)
        pieces.append(jnp.where(sub == CODE_ROW, codes, s))
    stats = jnp.concatenate(pieces, axis=0).astype(BF16)
    for i in range(owners):
        out_ref[i, MOST * block_rows :, :] = stats


def receive_kernel(
    arr_ref, y_ref, out_hbm, loss_ref, out_ref, wide, scale, code_v, code_s, acc, bias, code_sem, out_sem
):
    owners = arr_ref.shape[0]
    halves, width, _ = y_ref.shape
    tiles = width // LANES
    block_rows = halves * BLK
    span = width + BLK
    vocab_width = float(width * owners)
    me = lax.axis_index("vocab")

    for h in range(halves):

        @pl.loop(0, width // 512)
        def _(i):
            acc[pl.ds(pl.multiple_of(h * span + i * 512, BLK), 512), :] = jnp.full((512, LANES), TINY, F32)

    wide[...] = arr_ref[:, MOST * block_rows :, :].astype(F32).reshape(owners * TAIL_ROWS, LANES)
    codes = wide[pl.ds(CODE_ROW, owners, stride=TAIL_ROWS), :].astype(jnp.int32)
    code_v[...] = jnp.where(codes < 0, width // BLK, codes)
    code_copy = pltpu.make_async_copy(code_v, code_s, code_sem)
    code_copy.start()

    row_terms = jnp.zeros((1, LANES), F32)
    for h in range(halves):

        def stat(i):
            return wide[pl.ds(8 * h + i, owners, stride=TAIL_ROWS), :]

        t_high = stat(0)
        t_top = jnp.max(t_high, axis=0, keepdims=True)
        t_rel = jnp.exp2((t_high - t_top) * EXP2_SCALE)
        inv = vocab_width / jnp.sum(t_rel * (stat(1) + stat(2)), axis=0, keepdims=True)
        scale_h = t_rel * inv
        scale[h * owners : (h + 1) * owners, :] = scale_h
        total = jnp.sum(scale_h * (stat(3) + stat(4)), axis=0, keepdims=True)
        log_total = jnp.log2(total)
        s_lse = stat(5) + stat(6)
        s_top = jnp.max(s_lse, axis=0, keepdims=True)
        lse = s_top + jnp.log2(jnp.sum(jnp.exp2(s_lse - s_top), axis=0, keepdims=True))
        bias[h : h + 1, :] = lse - log_total
        row_terms = row_terms + total * (log_total - math.log2(vocab_width)) * (1.0 / owners)

    code_copy.wait()

    def add_source(src, carry):
        for slot in range(MOST):
            c = code_s[src, me * MOST + slot]
            for h in range(halves):
                at = pl.ds(pl.multiple_of(h * span + c * BLK, BLK), BLK)
                lo = slot * block_rows + h * BLK
                term = arr_ref[src, lo : lo + BLK, :].astype(F32)
                acc[at, :] = acc[at, :] + term * scale[pl.ds(h * owners + src, 1), :]
        return carry

    lax.fori_loop(0, owners, add_source, 0, unroll=4)

    chunks = out_sem.shape[0]
    chunk = width // chunks

    def tile(t, loss):
        cols = pl.ds(pl.multiple_of(t * LANES, LANES), LANES)
        for h in range(halves):
            lanes = slice(h * LANES, (h + 1) * LANES)
            target = acc[pl.ds(pl.multiple_of(h * span + t * LANES, BLK), LANES), :]
            goal = y_ref[h, cols, :].astype(F32) * EXP2_SCALE - bias[h : h + 1, :]
            out_ref[lanes, cols] = (jnp.exp2(goal) - target).astype(BF16).T
            term = target * (jnp.log2(target) - goal)
            loss = loss + jnp.sum(term.reshape(LANES // 32, 32, LANES), axis=0)
        return loss

    loss = jnp.zeros((32, LANES), F32)
    out_copies = []
    for i in range(chunks):
        per_chunk = tiles // chunks
        loss = lax.fori_loop(i * per_chunk, (i + 1) * per_chunk, tile, loss, unroll=True)
        part = pl.ds(i * chunk, chunk)
        copy = pltpu.make_async_copy(out_ref.at[:, part], out_hbm.at[:, part], out_sem.at[i])
        copy.start()
        out_copies.append(copy)
    loss_ref[...] = jnp.broadcast_to(
        (jnp.sum(loss, axis=0, keepdims=True) + row_terms).reshape(1, 1, LANES), loss_ref.shape
    )
    for copy in out_copies:
        copy.wait()


def per_device(mentor_score_matrix, learner_score_matrix, align_dev, align_slot, align_weight):
    owners = lax.axis_size("vocab")
    shards = owners * lax.axis_size("dp")
    rows, teacher_width = mentor_score_matrix.shape
    width = learner_score_matrix.shape[1]
    tb_local, topk = align_dev.shape
    halves = rows // LANES
    block_rows = halves * BLK
    packet_rows = MOST * block_rows + TAIL_ROWS
    chunks = BLK * BLK // LANES
    weight = (
        align_weight.reshape(tb_local, topk, chunks, LANES)
        .transpose(0, 2, 1, 3)
        .reshape(tb_local * chunks * topk, LANES)
    )
    vmem = pl.BlockSpec(memory_space=pltpu.VMEM)
    hbm = pl.BlockSpec(memory_space=pltpu.HBM)
    params = pltpu.CompilerParams(vmem_limit_bytes=20 * 2**20)
    outgoing, learner_t = pl.pallas_call(
        send_kernel,
        out_shape=(
            jax.ShapeDtypeStruct((owners, packet_rows, LANES), BF16),
            jax.ShapeDtypeStruct((halves, width, LANES), BF16),
        ),
        in_specs=[hbm] * 5,
        out_specs=(vmem, vmem),
        scratch_shapes=[
            pltpu.VMEM((topk, tb_local), jnp.int32),
            pltpu.VMEM((topk, tb_local), jnp.int32),
            pltpu.VMEM((rows, teacher_width), BF16),
            pltpu.VMEM(weight.shape, BF16),
            pltpu.VMEM((rows, width), BF16),
            pltpu.VMEM((teacher_width // LANES, rows, LANES), BF16),
            pltpu.VMEM((halves, LANES, LANES), F32),
            pltpu.VMEM((8, LANES), F32),
            pltpu.VMEM((32, LANES), jnp.int32),
            pltpu.SMEM((32, LANES), jnp.int32),
            pltpu.SemaphoreType.DMA,
            pltpu.SemaphoreType.DMA,
            pltpu.SemaphoreType.DMA,
            pltpu.SemaphoreType.DMA,
            pltpu.SemaphoreType.DMA((halves,)),
            pltpu.SemaphoreType.DMA,
        ],
        compiler_params=params,
        name="send",
    )(*(
        pltpu.with_memory_space_constraint(a, pltpu.HBM)
        for a in (align_dev.T, align_slot.T, mentor_score_matrix, learner_score_matrix, weight)
    ))
    arrived = lax.all_to_all(outgoing, "vocab", split_axis=0, concat_axis=0, tiled=True)
    scaled_grad, loss = pl.pallas_call(
        receive_kernel,
        out_shape=(
            jax.ShapeDtypeStruct((rows, width), BF16),
            jax.ShapeDtypeStruct((shards, 1, LANES), F32),
        ),
        in_specs=[vmem, vmem],
        out_specs=(hbm, vmem),
        scratch_shapes=[
            pltpu.VMEM((rows, width), BF16),
            pltpu.VMEM((owners * TAIL_ROWS, LANES), F32),
            pltpu.VMEM((halves * owners, LANES), F32),
            pltpu.VMEM((owners, LANES), jnp.int32),
            pltpu.SMEM((owners, LANES), jnp.int32),
            pltpu.VMEM((halves * (width + BLK), LANES), F32),
            pltpu.VMEM((8, LANES), F32),
            pltpu.SemaphoreType.DMA,
            pltpu.SemaphoreType.DMA((8,)),
        ],
        compiler_params=params,
        name="receive",
    )(arrived, learner_t)
    parts = lax.all_to_all(loss, ("dp", "vocab"), split_axis=0, concat_axis=0, tiled=True)
    tokens = float(rows * lax.axis_size("dp"))
    unit = math.log(2.0) / (width * owners)
    divergence = SMOOTHING_HEAT * SMOOTHING_HEAT * unit / tokens * jnp.sum(parts)
    return scaled_grad, divergence


def solution(mesh):
    in_specs = (
        P("dp", "vocab"),
        P("dp", "vocab"),
        P("vocab", None),
        P("vocab", None),
        P("vocab", None, None),
    )
    out_specs = (P("dp", "vocab"), P())
    return jax.shard_map(
        per_device, mesh=mesh, in_specs=in_specs, out_specs=out_specs, check_vma=False
    )
```

```python
import math

import jax
import jax.numpy as jnp
from jax import lax
from jax.experimental import pallas as pl
from jax.experimental.pallas import tpu as pltpu
from jax.sharding import PartitionSpec as P

BLK = 64
LANES = 128
SMOOTHING_HEAT = 2
MOST = 2
TAIL_ROWS = 16
CODE_ROW = 7
EXP2_SCALE = math.log2(math.e) / SMOOTHING_HEAT
TINY = 2.0**-126

F32 = jnp.float32
BF16 = jnp.bfloat16


def split2(x):
    hi = x.astype(BF16).astype(F32)
    return hi, x - hi


def send_kernel(
    dev_hbm, slot_hbm, x_hbm, y_hbm, w_hbm, out_ref, yt_ref, acc_ref, dev_ref, slot_ref, x_ref, w_ref, y_ref,
    probs, high_v, edge_v, pos_v, pos_s, dev_sem, slot_sem, y_sem, pos_sem, x_sem, w_sem,
):
    rows, width = x_ref.shape
    owners = out_ref.shape[0]
    halves = rows // LANES
    pairs = width // LANES
    student_tiles = y_ref.shape[1] // LANES
    topk, blocks = dev_ref.shape
    block_rows = halves * BLK
    padded = pos_v.shape[0]

    def x_copy(h):
        lanes = pl.ds(h * LANES, LANES)
        return pltpu.make_async_copy(x_hbm.at[lanes], x_ref.at[lanes], x_sem.at[h])

    dev_copy = pltpu.make_async_copy(dev_hbm, dev_ref, dev_sem)
    dev_copy.start()
    slot_copy = pltpu.make_async_copy(slot_hbm, slot_ref, slot_sem)
    slot_copy.start()
    for h in range(halves):
        x_copy(h).start()
    y_copy = pltpu.make_async_copy(y_hbm, y_ref, y_sem)
    y_copy.start()
    w_copy = pltpu.make_async_copy(w_hbm, w_ref, w_sem)
    w_copy.start()

    edge_v[...] = jnp.full((8, LANES), -1.0, F32)
    dev_copy.wait()
    slot_copy.wait()
    edge_v[:topk, :blocks] = dev_ref[...].astype(F32)
    edge_v[topk : 2 * topk, :blocks] = slot_ref[...].astype(F32)
    edge_rows = edge_v[...]
    edge_cols = edge_rows.T[:padded]
    below = lax.broadcasted_iota(jnp.int32, (padded, LANES), 1) < lax.broadcasted_iota(
        jnp.int32, (padded, LANES), 0
    )
    edge_lane = lax.broadcasted_iota(jnp.int32, (padded, LANES), 1)
    code = jnp.zeros((padded, LANES), F32)
    places = jnp.zeros((padded, LANES), F32)
    for k in range(topk):
        owner = edge_cols[:, k : k + 1]
        hits = jnp.zeros((padded, LANES), F32)
        for other in range(topk):
            same = (owner == edge_rows[other : other + 1, :]) & below
            hits = hits + jnp.where(same, 1.0, 0.0)
        place = owner * MOST + jnp.sum(hits, axis=1, keepdims=True)
        code = code + jnp.where(
            place == edge_lane.astype(F32), edge_cols[:, topk + k : topk + k + 1] + 1.0, 0.0
        )
        places = jnp.where(edge_lane == k, place, places)
    codes = jnp.sum(code, axis=0, keepdims=True) - 1.0
    pos_v[...] = places.astype(jnp.int32)
    pos_copy = pltpu.make_async_copy(pos_v, pos_s, pos_sem)
    pos_copy.start()

    def shard_max(ref, h, tiles):
        lanes = slice(h * LANES, (h + 1) * LANES)
        m = ref[lanes, :LANES]
        for t in range(1, tiles):
            m = jnp.maximum(m, ref[lanes, t * LANES : (t + 1) * LANES])
        return jnp.max(m.astype(F32), axis=1, keepdims=True)

    acc_ref[...] = jnp.full(acc_ref.shape, TINY, F32)
    for h in range(halves):
        x_copy(h).wait()
    teacher_high, teacher_sum = [], []
    for h in range(halves):
        lanes = slice(h * LANES, (h + 1) * LANES)
        high = shard_max(x_ref, h, pairs)
        high_b = jnp.broadcast_to(high, (LANES, LANES))
        total = jnp.zeros((LANES, LANES), F32)
        for q in range(pairs):
            e = jnp.exp2((x_ref[lanes, q * LANES : (q + 1) * LANES].astype(F32) - high_b) * EXP2_SCALE)
            total = total + e
            probs[q, lanes, :] = e.astype(BF16)
        teacher_high.append(high)
        teacher_sum.append(jnp.sum(total, axis=1, keepdims=True))

    y_copy.wait()
    w_copy.wait()
    student_high = [shard_max(y_ref, h, student_tiles) for h in range(halves)]

    pos_copy.wait()

    for h in range(halves):
        high_v[h] = jnp.broadcast_to(student_high[h], (LANES, LANES))
    lane = lax.broadcasted_iota(jnp.int32, (BLK, LANES), 1)
    even = lane % 2 == 0
    first = lane < BLK
    mass = jnp.zeros((8, rows), F32)
    student_total = [jnp.zeros((LANES, LANES), F32) for _ in range(halves)]
    items = [(h, t) for h in range(halves) for t in range(student_tiles)]
    for q in range(pairs):
        w = w_ref[q * LANES : (q + 1) * LANES, :].astype(F32).T
        a0, a1 = w[:BLK], w[BLK:]
        l0 = jnp.where(even, a0, pltpu.roll(a1, 1, 1))
        l1 = jnp.where(even, pltpu.roll(a0, LANES - 1, 1), a1)
        lhs = jnp.concatenate(
            [
                jnp.where(first, l0, 0.0),
                jnp.where(first, l1, 0.0),
                jnp.where(first, 0.0, l0),
                jnp.where(first, 0.0, l1),
            ],
            axis=0,
        ).astype(BF16)
        u = lax.dot_general(
            lhs, probs[q], (((1,), (1,)), ((), ())), preferred_element_type=F32
        )
        for h, t in items[len(items) * q // pairs : len(items) * (q + 1) // pairs]:
            y = y_ref[h * LANES : (h + 1) * LANES, t * LANES : (t + 1) * LANES].astype(F32)
            student_total[h] = student_total[h] + jnp.exp2((y - high_v[h]) * EXP2_SCALE)
            yt_ref[h, t * LANES : (t + 1) * LANES, :] = y_ref[
                h * LANES : (h + 1) * LANES, t * LANES : (t + 1) * LANES
            ].T
        mass = mass + jnp.sum(u.reshape(4 * BLK // 8, 8, rows), axis=0)
        u = u.astype(BF16)
        for edge in range(2 * topk):
            place = pos_s[2 * q + edge // topk, edge % topk]
            at = pl.multiple_of((place % MOST) * block_rows, block_rows)
            for h in range(halves):
                out_ref[place // MOST, pl.ds(at + h * BLK, BLK), :] = u[
                    edge * BLK : (edge + 1) * BLK, h * LANES : (h + 1) * LANES
                ]

    row_lane = lax.broadcasted_iota(jnp.int32, (LANES, LANES), 1)
    r_hi, r_lo = split2(jnp.sum(mass, axis=0, keepdims=True))
    sub = lax.broadcasted_iota(jnp.int32, (8, LANES), 0)
    pieces = []
    for h in range(halves):
        t_hi, t_lo = split2(teacher_sum[h])
        student_sum = jnp.sum(student_total[h], axis=1, keepdims=True)
        s_hi, s_lo = split2(student_high[h] * EXP2_SCALE + jnp.log2(student_sum))
        columns = jnp.zeros((LANES, LANES), F32)
        for i, v in ((0, teacher_high[h]), (1, t_hi), (2, t_lo), (5, s_hi), (6, s_lo)):
            columns = jnp.where(row_lane == i, v, columns)
        lanes = slice(h * LANES, (h + 1) * LANES)
        s = columns.T[:8]
        s = jnp.where(sub == 3, r_hi[:, lanes], s)
        s = jnp.where(sub == 4, r_lo[:, lanes], s)
        pieces.append(jnp.where(sub == CODE_ROW, codes, s))
    stats = jnp.concatenate(pieces, axis=0).astype(BF16)
    for i in range(owners):
        out_ref[i, MOST * block_rows :, :] = stats


def receive_kernel(
    arr_ref, y_ref, acc_in, out_hbm, loss_ref, acc, out_ref, wide, scale, code_v, code_s, bias, code_sem,
    out_sem,
):
    owners = arr_ref.shape[0]
    halves, width, _ = y_ref.shape
    tiles = width // LANES
    block_rows = halves * BLK
    span = width + BLK
    vocab_width = float(width * owners)
    me = lax.axis_index("vocab")

    wide[...] = arr_ref[:, MOST * block_rows :, :].astype(F32).reshape(owners * TAIL_ROWS, LANES)
    codes = wide[pl.ds(CODE_ROW, owners, stride=TAIL_ROWS), :].astype(jnp.int32)
    code_v[...] = jnp.where(codes < 0, width // BLK, codes)
    code_copy = pltpu.make_async_copy(code_v, code_s, code_sem)
    code_copy.start()

    row_terms = jnp.zeros((1, LANES), F32)
    for h in range(halves):

        def stat(i):
            return wide[pl.ds(8 * h + i, owners, stride=TAIL_ROWS), :]

        t_high = stat(0)
        t_top = jnp.max(t_high, axis=0, keepdims=True)
        t_rel = jnp.exp2((t_high - t_top) * EXP2_SCALE)
        inv = vocab_width / jnp.sum(t_rel * (stat(1) + stat(2)), axis=0, keepdims=True)
        scale_h = t_rel * inv
        scale[h * owners : (h + 1) * owners, :] = scale_h
        total = jnp.sum(scale_h * (stat(3) + stat(4)), axis=0, keepdims=True)
        log_total = jnp.log2(total)
        s_lse = stat(5) + stat(6)
        s_top = jnp.max(s_lse, axis=0, keepdims=True)
        lse = s_top + jnp.log2(jnp.sum(jnp.exp2(s_lse - s_top), axis=0, keepdims=True))
        bias[h : h + 1, :] = lse - log_total
        row_terms = row_terms + total * (log_total - math.log2(vocab_width)) * (1.0 / owners)

    code_copy.wait()

    def add_source(src, carry):
        for slot in range(MOST):
            c = code_s[src, me * MOST + slot]
            for h in range(halves):
                at = pl.ds(pl.multiple_of(h * span + c * BLK, BLK), BLK)
                lo = slot * block_rows + h * BLK
                term = arr_ref[src, lo : lo + BLK, :].astype(F32)
                acc[at, :] = acc[at, :] + term * scale[pl.ds(h * owners + src, 1), :]
        return carry

    lax.fori_loop(0, owners, add_source, 0, unroll=4)

    chunks = out_sem.shape[0]
    chunk = width // chunks

    def tile(t, loss):
        cols = pl.ds(pl.multiple_of(t * LANES, LANES), LANES)
        for h in range(halves):
            lanes = slice(h * LANES, (h + 1) * LANES)
            target = acc[pl.ds(pl.multiple_of(h * span + t * LANES, BLK), LANES), :]
            goal = y_ref[h, cols, :].astype(F32) * EXP2_SCALE - bias[h : h + 1, :]
            out_ref[lanes, cols] = (jnp.exp2(goal) - target).astype(BF16).T
            term = target * (jnp.log2(target) - goal)
            loss = loss + jnp.sum(term.reshape(LANES // 32, 32, LANES), axis=0)
        return loss

    loss = jnp.zeros((32, LANES), F32)
    out_copies = []
    for i in range(chunks):
        per_chunk = tiles // chunks
        loss = lax.fori_loop(i * per_chunk, (i + 1) * per_chunk, tile, loss, unroll=True)
        part = pl.ds(i * chunk, chunk)
        copy = pltpu.make_async_copy(out_ref.at[:, part], out_hbm.at[:, part], out_sem.at[i])
        copy.start()
        out_copies.append(copy)
    loss_ref[...] = jnp.broadcast_to(
        (jnp.sum(loss, axis=0, keepdims=True) + row_terms).reshape(1, 1, LANES), loss_ref.shape
    )
    for copy in out_copies:
        copy.wait()


def per_device(mentor_score_matrix, learner_score_matrix, align_dev, align_slot, align_weight):
    owners = lax.axis_size("vocab")
    shards = owners * lax.axis_size("dp")
    rows, teacher_width = mentor_score_matrix.shape
    width = learner_score_matrix.shape[1]
    tb_local, topk = align_dev.shape
    halves = rows // LANES
    block_rows = halves * BLK
    packet_rows = MOST * block_rows + TAIL_ROWS
    chunks = BLK * BLK // LANES
    weight = (
        align_weight.reshape(tb_local, topk, chunks, LANES)
        .transpose(0, 2, 1, 3)
        .reshape(tb_local * chunks * topk, LANES)
    )
    vmem = pl.BlockSpec(memory_space=pltpu.VMEM)
    hbm = pl.BlockSpec(memory_space=pltpu.HBM)
    params = pltpu.CompilerParams(vmem_limit_bytes=20 * 2**20)
    acc_shape = (halves * (width + BLK), LANES)
    outgoing, learner_t, target = pl.pallas_call(
        send_kernel,
        out_shape=(
            jax.ShapeDtypeStruct((owners, packet_rows, LANES), BF16),
            jax.ShapeDtypeStruct((halves, width, LANES), BF16),
            jax.ShapeDtypeStruct(acc_shape, F32),
        ),
        in_specs=[hbm] * 5,
        out_specs=(vmem, vmem, vmem),
        scratch_shapes=[
            pltpu.VMEM((topk, tb_local), jnp.int32),
            pltpu.VMEM((topk, tb_local), jnp.int32),
            pltpu.VMEM((rows, teacher_width), BF16),
            pltpu.VMEM(weight.shape, BF16),
            pltpu.VMEM((rows, width), BF16),
            pltpu.VMEM((teacher_width // LANES, rows, LANES), BF16),
            pltpu.VMEM((halves, LANES, LANES), F32),
            pltpu.VMEM((8, LANES), F32),
            pltpu.VMEM((32, LANES), jnp.int32),
            pltpu.SMEM((32, LANES), jnp.int32),
            pltpu.SemaphoreType.DMA,
            pltpu.SemaphoreType.DMA,
            pltpu.SemaphoreType.DMA,
            pltpu.SemaphoreType.DMA,
            pltpu.SemaphoreType.DMA((halves,)),
            pltpu.SemaphoreType.DMA,
        ],
        compiler_params=params,
        name="send",
    )(*(
        pltpu.with_memory_space_constraint(a, pltpu.HBM)
        for a in (align_dev.T, align_slot.T, mentor_score_matrix, learner_score_matrix, weight)
    ))
    arrived = lax.all_to_all(outgoing, "vocab", split_axis=0, concat_axis=0, tiled=True)
    scaled_grad, loss, _ = pl.pallas_call(
        receive_kernel,
        out_shape=(
            jax.ShapeDtypeStruct((rows, width), BF16),
            jax.ShapeDtypeStruct((shards, 1, LANES), F32),
            jax.ShapeDtypeStruct(acc_shape, F32),
        ),
        in_specs=[vmem, vmem, vmem],
        out_specs=(hbm, vmem, vmem),
        input_output_aliases={2: 2},
        scratch_shapes=[
            pltpu.VMEM((rows, width), BF16),
            pltpu.VMEM((owners * TAIL_ROWS, LANES), F32),
            pltpu.VMEM((halves * owners, LANES), F32),
            pltpu.VMEM((owners, LANES), jnp.int32),
            pltpu.SMEM((owners, LANES), jnp.int32),
            pltpu.VMEM((8, LANES), F32),
            pltpu.SemaphoreType.DMA,
            pltpu.SemaphoreType.DMA((8,)),
        ],
        compiler_params=params,
        name="receive",
    )(arrived, learner_t, target)
    parts = lax.all_to_all(loss, ("dp", "vocab"), split_axis=0, concat_axis=0, tiled=True)
    tokens = float(rows * lax.axis_size("dp"))
    unit = math.log(2.0) / (width * owners)
    divergence = SMOOTHING_HEAT * SMOOTHING_HEAT * unit / tokens * jnp.sum(parts)
    return scaled_grad, divergence


def solution(mesh):
    in_specs = (
        P("dp", "vocab"),
        P("dp", "vocab"),
        P("vocab", None),
        P("vocab", None),
        P("vocab", None, None),
    )
    out_specs = (P("dp", "vocab"), P())
    return jax.shard_map(
        per_device, mesh=mesh, in_specs=in_specs, out_specs=out_specs, check_vma=False
    )
```

```python
import functools
import math

import jax
import jax.numpy as jnp
from jax import lax
from jax.experimental import pallas as pl
from jax.experimental.pallas import tpu as pltpu
from jax.sharding import PartitionSpec as P

BLK = 64
LANES = 128
SMOOTHING_HEAT = 2
MOST = 2
TAIL_ROWS = 16
CODE_ROW = 7
EXP2_SCALE = math.log2(math.e) / SMOOTHING_HEAT
TINY = 2.0**-126

F32 = jnp.float32
BF16 = jnp.bfloat16


def split2(x):
    hi = x.astype(BF16).astype(F32)
    return hi, x - hi


def send_kernel(
    dev_hbm, slot_hbm, x_hbm, y_hbm, w_hbm, out_ref, yt_ref, acc_lo, acc_hi, dev_ref, slot_ref, x_ref, w_ref, y_ref,
    probs, high_v, edge_v, pos_v, pos_s, dev_sem, slot_sem, y_sem, pos_sem, x_sem, w_sem,
):
    rows, width = x_ref.shape
    owners = out_ref.shape[0]
    halves = rows // LANES
    pairs = width // LANES
    student_tiles = y_ref.shape[1] // LANES
    topk, blocks = dev_ref.shape
    block_rows = halves * BLK
    padded = pos_v.shape[0]

    def x_copy(h):
        lanes = pl.ds(h * LANES, LANES)
        return pltpu.make_async_copy(x_hbm.at[lanes], x_ref.at[lanes], x_sem.at[h])

    dev_copy = pltpu.make_async_copy(dev_hbm, dev_ref, dev_sem)
    dev_copy.start()
    slot_copy = pltpu.make_async_copy(slot_hbm, slot_ref, slot_sem)
    slot_copy.start()
    for h in range(halves):
        x_copy(h).start()
    y_copy = pltpu.make_async_copy(y_hbm, y_ref, y_sem)
    y_copy.start()
    w_copy = pltpu.make_async_copy(w_hbm, w_ref, w_sem)
    w_copy.start()

    edge_v[...] = jnp.full((8, LANES), -1.0, F32)
    dev_copy.wait()
    slot_copy.wait()
    edge_v[:topk, :blocks] = dev_ref[...].astype(F32)
    edge_v[topk : 2 * topk, :blocks] = slot_ref[...].astype(F32)
    edge_rows = edge_v[...]
    edge_cols = edge_rows.T[:padded]
    below = lax.broadcasted_iota(jnp.int32, (padded, LANES), 1) < lax.broadcasted_iota(
        jnp.int32, (padded, LANES), 0
    )
    edge_lane = lax.broadcasted_iota(jnp.int32, (padded, LANES), 1)
    code = jnp.zeros((padded, LANES), F32)
    places = jnp.zeros((padded, LANES), F32)
    for k in range(topk):
        owner = edge_cols[:, k : k + 1]
        hits = jnp.zeros((padded, LANES), F32)
        for other in range(topk):
            same = (owner == edge_rows[other : other + 1, :]) & below
            hits = hits + jnp.where(same, 1.0, 0.0)
        place = owner * MOST + jnp.sum(hits, axis=1, keepdims=True)
        code = code + jnp.where(
            place == edge_lane.astype(F32), edge_cols[:, topk + k : topk + k + 1] + 1.0, 0.0
        )
        places = jnp.where(edge_lane == k, place, places)
    codes = jnp.sum(code, axis=0, keepdims=True) - 1.0
    pos_v[...] = places.astype(jnp.int32)
    pos_copy = pltpu.make_async_copy(pos_v, pos_s, pos_sem)
    pos_copy.start()

    def shard_max(ref, h, tiles):
        lanes = slice(h * LANES, (h + 1) * LANES)
        m = ref[lanes, :LANES]
        for t in range(1, tiles):
            m = jnp.maximum(m, ref[lanes, t * LANES : (t + 1) * LANES])
        return jnp.max(m.astype(F32), axis=1, keepdims=True)

    for acc in (acc_lo, acc_hi):
        acc[...] = jnp.full(acc.shape, TINY, F32)
    for h in range(halves):
        x_copy(h).wait()
    teacher_high, teacher_sum = [], []
    for h in range(halves):
        lanes = slice(h * LANES, (h + 1) * LANES)
        high = shard_max(x_ref, h, pairs)
        high_b = jnp.broadcast_to(high, (LANES, LANES))
        total = jnp.zeros((LANES, LANES), F32)
        for q in range(pairs):
            e = jnp.exp2((x_ref[lanes, q * LANES : (q + 1) * LANES].astype(F32) - high_b) * EXP2_SCALE)
            total = total + e
            probs[q, lanes, :] = e.astype(BF16)
        teacher_high.append(high)
        teacher_sum.append(jnp.sum(total, axis=1, keepdims=True))

    y_copy.wait()
    w_copy.wait()
    student_high = [shard_max(y_ref, h, student_tiles) for h in range(halves)]

    pos_copy.wait()

    for h in range(halves):
        high_v[h] = jnp.broadcast_to(student_high[h], (LANES, LANES))
    lane = lax.broadcasted_iota(jnp.int32, (BLK, LANES), 1)
    even = lane % 2 == 0
    first = lane < BLK
    mass = jnp.zeros((8, rows), F32)
    student_total = [jnp.zeros((LANES, LANES), F32) for _ in range(halves)]
    items = [(h, t) for h in range(halves) for t in range(student_tiles)]
    for q in range(pairs):
        w = w_ref[q * LANES : (q + 1) * LANES, :].astype(F32).T
        a0, a1 = w[:BLK], w[BLK:]
        l0 = jnp.where(even, a0, pltpu.roll(a1, 1, 1))
        l1 = jnp.where(even, pltpu.roll(a0, LANES - 1, 1), a1)
        lhs = jnp.concatenate(
            [
                jnp.where(first, l0, 0.0),
                jnp.where(first, l1, 0.0),
                jnp.where(first, 0.0, l0),
                jnp.where(first, 0.0, l1),
            ],
            axis=0,
        ).astype(BF16)
        u = lax.dot_general(
            lhs, probs[q], (((1,), (1,)), ((), ())), preferred_element_type=F32
        )
        for h, t in items[len(items) * q // pairs : len(items) * (q + 1) // pairs]:
            y = y_ref[h * LANES : (h + 1) * LANES, t * LANES : (t + 1) * LANES].astype(F32)
            student_total[h] = student_total[h] + jnp.exp2((y - high_v[h]) * EXP2_SCALE)
            yt_ref[h, t * LANES : (t + 1) * LANES, :] = y_ref[
                h * LANES : (h + 1) * LANES, t * LANES : (t + 1) * LANES
            ].T
        mass = mass + jnp.sum(u.reshape(4 * BLK // 8, 8, rows), axis=0)
        u = u.astype(BF16)
        for edge in range(2 * topk):
            place = pos_s[2 * q + edge // topk, edge % topk]
            at = pl.multiple_of((place % MOST) * block_rows, block_rows)
            for h in range(halves):
                out_ref[place // MOST, pl.ds(at + h * BLK, BLK), :] = u[
                    edge * BLK : (edge + 1) * BLK, h * LANES : (h + 1) * LANES
                ]

    row_lane = lax.broadcasted_iota(jnp.int32, (LANES, LANES), 1)
    r_hi, r_lo = split2(jnp.sum(mass, axis=0, keepdims=True))
    sub = lax.broadcasted_iota(jnp.int32, (8, LANES), 0)
    pieces = []
    for h in range(halves):
        t_hi, t_lo = split2(teacher_sum[h])
        student_sum = jnp.sum(student_total[h], axis=1, keepdims=True)
        s_hi, s_lo = split2(student_high[h] * EXP2_SCALE + jnp.log2(student_sum))
        columns = jnp.zeros((LANES, LANES), F32)
        for i, v in ((0, teacher_high[h]), (1, t_hi), (2, t_lo), (5, s_hi), (6, s_lo)):
            columns = jnp.where(row_lane == i, v, columns)
        lanes = slice(h * LANES, (h + 1) * LANES)
        s = columns.T[:8]
        s = jnp.where(sub == 3, r_hi[:, lanes], s)
        s = jnp.where(sub == 4, r_lo[:, lanes], s)
        pieces.append(jnp.where(sub == CODE_ROW, codes, s))
    stats = jnp.concatenate(pieces, axis=0).astype(BF16)
    for i in range(owners):
        out_ref[i, MOST * block_rows :, :] = stats


def receive_kernel(
    arr_ref, y_ref, lo_in, hi_in, out_hbm, loss_ref, acc_lo, acc_hi, out_ref, wide, scale, code_v, code_s,
    bias, code_sem, out_sem,
):
    owners = arr_ref.shape[0]
    halves, width, _ = y_ref.shape
    tiles = width // LANES
    block_rows = halves * BLK
    accs = (acc_lo, acc_hi)
    vocab_width = float(width * owners)
    me = lax.axis_index("vocab")

    wide[...] = arr_ref[:, MOST * block_rows :, :].astype(F32).reshape(owners * TAIL_ROWS, LANES)
    codes = wide[pl.ds(CODE_ROW, owners, stride=TAIL_ROWS), :].astype(jnp.int32)
    code_v[...] = jnp.where(codes < 0, width // BLK, codes)
    code_copy = pltpu.make_async_copy(code_v, code_s, code_sem)
    code_copy.start()

    row_terms = jnp.zeros((1, LANES), F32)
    for h in range(halves):

        def stat(i):
            return wide[pl.ds(8 * h + i, owners, stride=TAIL_ROWS), :]

        t_high = stat(0)
        t_top = jnp.max(t_high, axis=0, keepdims=True)
        t_rel = jnp.exp2((t_high - t_top) * EXP2_SCALE)
        inv = vocab_width / jnp.sum(t_rel * (stat(1) + stat(2)), axis=0, keepdims=True)
        scale_h = t_rel * inv
        scale[h * owners : (h + 1) * owners, :] = scale_h
        total = jnp.sum(scale_h * (stat(3) + stat(4)), axis=0, keepdims=True)
        log_total = jnp.log2(total)
        s_lse = stat(5) + stat(6)
        s_top = jnp.max(s_lse, axis=0, keepdims=True)
        lse = s_top + jnp.log2(jnp.sum(jnp.exp2(s_lse - s_top), axis=0, keepdims=True))
        bias[h : h + 1, :] = lse - log_total
        row_terms = row_terms + total * (log_total - math.log2(vocab_width)) * (1.0 / owners)

    code_copy.wait()

    def add_source(src, carry):
        for slot in range(MOST):
            c = code_s[src, me * MOST + slot]
            for h in range(halves):
                acc, at = accs[h], pl.ds(pl.multiple_of(c * BLK, BLK), BLK)
                lo = slot * block_rows + h * BLK
                term = arr_ref[src, lo : lo + BLK, :].astype(F32)
                acc[at, :] = acc[at, :] + term * scale[pl.ds(h * owners + src, 1), :]
        return carry

    lax.fori_loop(0, owners, add_source, 0, unroll=4)

    chunks = out_sem.shape[0]
    chunk = width // chunks

    def tile(t, loss):
        cols = pl.ds(pl.multiple_of(t * LANES, LANES), LANES)
        for h in range(halves):
            lanes = slice(h * LANES, (h + 1) * LANES)
            target = accs[h][cols, :]
            goal = y_ref[h, cols, :].astype(F32) * EXP2_SCALE - bias[h : h + 1, :]
            out_ref[lanes, cols] = (jnp.exp2(goal) - target).astype(BF16).T
            term = target * (jnp.log2(target) - goal)
            loss = loss + jnp.sum(term.reshape(LANES // 32, 32, LANES), axis=0)
        return loss

    loss = jnp.zeros((32, LANES), F32)
    out_copies = []
    for i in range(chunks):
        per_chunk = tiles // chunks
        loss = lax.fori_loop(i * per_chunk, (i + 1) * per_chunk, tile, loss, unroll=True)
        part = pl.ds(i * chunk, chunk)
        copy = pltpu.make_async_copy(out_ref.at[:, part], out_hbm.at[:, part], out_sem.at[i])
        copy.start()
        out_copies.append(copy)
    loss_ref[...] = jnp.broadcast_to(
        (jnp.sum(loss, axis=0, keepdims=True) + row_terms).reshape(1, 1, LANES), loss_ref.shape
    )
    for copy in out_copies:
        copy.wait()


def total_kernel(factor, parts_ref, out_ref):
    out_ref[0] = jnp.sum(parts_ref[...]) * factor


def per_device(mentor_score_matrix, learner_score_matrix, align_dev, align_slot, align_weight):
    owners = lax.axis_size("vocab")
    shards = owners * lax.axis_size("dp")
    rows, teacher_width = mentor_score_matrix.shape
    width = learner_score_matrix.shape[1]
    tb_local, topk = align_dev.shape
    halves = rows // LANES
    block_rows = halves * BLK
    packet_rows = MOST * block_rows + TAIL_ROWS
    chunks = BLK * BLK // LANES
    weight = (
        align_weight.reshape(tb_local, topk, chunks, LANES)
        .transpose(0, 2, 1, 3)
        .reshape(tb_local * chunks * topk, LANES)
    )
    vmem = pl.BlockSpec(memory_space=pltpu.VMEM)
    hbm = pl.BlockSpec(memory_space=pltpu.HBM)
    params = pltpu.CompilerParams(vmem_limit_bytes=20 * 2**20)
    acc_shape = (width + BLK, LANES)
    outgoing, learner_t, target_lo, target_hi = pl.pallas_call(
        send_kernel,
        out_shape=(
            jax.ShapeDtypeStruct((owners, packet_rows, LANES), BF16),
            jax.ShapeDtypeStruct((halves, width, LANES), BF16),
            jax.ShapeDtypeStruct(acc_shape, F32),
            jax.ShapeDtypeStruct(acc_shape, F32),
        ),
        in_specs=[hbm] * 5,
        out_specs=(vmem, vmem, vmem, vmem),
        scratch_shapes=[
            pltpu.VMEM((topk, tb_local), jnp.int32),
            pltpu.VMEM((topk, tb_local), jnp.int32),
            pltpu.VMEM((rows, teacher_width), BF16),
            pltpu.VMEM(weight.shape, BF16),
            pltpu.VMEM((rows, width), BF16),
            pltpu.VMEM((teacher_width // LANES, rows, LANES), BF16),
            pltpu.VMEM((halves, LANES, LANES), F32),
            pltpu.VMEM((8, LANES), F32),
            pltpu.VMEM((32, LANES), jnp.int32),
            pltpu.SMEM((32, LANES), jnp.int32),
            pltpu.SemaphoreType.DMA,
            pltpu.SemaphoreType.DMA,
            pltpu.SemaphoreType.DMA,
            pltpu.SemaphoreType.DMA,
            pltpu.SemaphoreType.DMA((halves,)),
            pltpu.SemaphoreType.DMA,
        ],
        compiler_params=params,
        name="send",
    )(*(
        pltpu.with_memory_space_constraint(a, pltpu.HBM)
        for a in (align_dev.T, align_slot.T, mentor_score_matrix, learner_score_matrix, weight)
    ))
    arrived = lax.all_to_all(outgoing, "vocab", split_axis=0, concat_axis=0, tiled=True)
    scaled_grad, loss, _, _ = pl.pallas_call(
        receive_kernel,
        out_shape=(
            jax.ShapeDtypeStruct((rows, width), BF16),
            jax.ShapeDtypeStruct((shards, 1, LANES), F32),
            jax.ShapeDtypeStruct(acc_shape, F32),
            jax.ShapeDtypeStruct(acc_shape, F32),
        ),
        in_specs=[vmem, vmem, vmem, vmem],
        out_specs=(hbm, vmem, vmem, vmem),
        input_output_aliases={2: 2, 3: 3},
        scratch_shapes=[
            pltpu.VMEM((rows, width), BF16),
            pltpu.VMEM((owners * TAIL_ROWS, LANES), F32),
            pltpu.VMEM((halves * owners, LANES), F32),
            pltpu.VMEM((owners, LANES), jnp.int32),
            pltpu.SMEM((owners, LANES), jnp.int32),
            pltpu.VMEM((8, LANES), F32),
            pltpu.SemaphoreType.DMA,
            pltpu.SemaphoreType.DMA((8,)),
        ],
        compiler_params=params,
        name="receive",
    )(arrived, learner_t, target_lo, target_hi)
    parts = lax.all_to_all(loss, ("dp", "vocab"), split_axis=0, concat_axis=0, tiled=True)
    tokens = float(rows * lax.axis_size("dp"))
    unit = math.log(2.0) / (width * owners)
    divergence = pl.pallas_call(
        functools.partial(total_kernel, SMOOTHING_HEAT * SMOOTHING_HEAT * unit / tokens),
        out_shape=jax.ShapeDtypeStruct((1,), F32),
        in_specs=[vmem],
        out_specs=pl.BlockSpec(memory_space=pltpu.SMEM),
        compiler_params=params,
        name="total",
    )(parts).reshape(())
    return scaled_grad, divergence


def solution(mesh):
    in_specs = (
        P("dp", "vocab"),
        P("dp", "vocab"),
        P("vocab", None),
        P("vocab", None),
        P("vocab", None, None),
    )
    out_specs = (P("dp", "vocab"), P())
    return jax.shard_map(
        per_device, mesh=mesh, in_specs=in_specs, out_specs=out_specs, check_vma=False
    )
```

```python
import functools
import math

import jax
import jax.numpy as jnp
from jax import lax
from jax.experimental import pallas as pl
from jax.experimental.pallas import tpu as pltpu
from jax.sharding import PartitionSpec as P

BLK = 64
LANES = 128
SMOOTHING_HEAT = 2
MOST = 2
TAIL_ROWS = 16
CODE_ROW = 7
EXP2_SCALE = math.log2(math.e) / SMOOTHING_HEAT
TINY = 2.0**-126

F32 = jnp.float32
BF16 = jnp.bfloat16


def split2(x):
    hi = x.astype(BF16).astype(F32)
    return hi, x - hi


def send_kernel(
    dev_hbm, slot_hbm, x_hbm, y_hbm, w_hbm, out_ref, yt_ref, acc_lo, acc_hi, dev_ref, slot_ref, x_ref, w_ref, y_ref,
    probs, high_v, edge_v, pos_v, pos_s, dev_sem, slot_sem, y_sem, pos_sem, x_sem, w_sem,
):
    rows, width = x_ref.shape
    owners = out_ref.shape[0]
    halves = rows // LANES
    pairs = width // LANES
    student_tiles = y_ref.shape[1] // LANES
    topk, blocks = dev_ref.shape
    block_rows = halves * BLK
    padded = pos_v.shape[0]

    def x_copy(h):
        lanes = pl.ds(h * LANES, LANES)
        return pltpu.make_async_copy(x_hbm.at[lanes], x_ref.at[lanes], x_sem.at[h])

    dev_copy = pltpu.make_async_copy(dev_hbm, dev_ref, dev_sem)
    dev_copy.start()
    slot_copy = pltpu.make_async_copy(slot_hbm, slot_ref, slot_sem)
    slot_copy.start()
    for h in range(halves):
        x_copy(h).start()
    y_copy = pltpu.make_async_copy(y_hbm, y_ref, y_sem)
    y_copy.start()
    w_copy = pltpu.make_async_copy(w_hbm, w_ref, w_sem)
    w_copy.start()

    edge_v[...] = jnp.full((8, LANES), -1.0, F32)
    dev_copy.wait()
    slot_copy.wait()
    edge_v[:topk, :blocks] = dev_ref[...].astype(F32)
    edge_v[topk : 2 * topk, :blocks] = slot_ref[...].astype(F32)
    edge_rows = edge_v[...]
    edge_cols = edge_rows.T[:padded]
    below = lax.broadcasted_iota(jnp.int32, (padded, LANES), 1) < lax.broadcasted_iota(
        jnp.int32, (padded, LANES), 0
    )
    edge_lane = lax.broadcasted_iota(jnp.int32, (padded, LANES), 1)
    code = jnp.zeros((padded, LANES), F32)
    places = jnp.zeros((padded, LANES), F32)
    for k in range(topk):
        owner = edge_cols[:, k : k + 1]
        hits = jnp.zeros((padded, LANES), F32)
        for other in range(topk):
            same = (owner == edge_rows[other : other + 1, :]) & below
            hits = hits + jnp.where(same, 1.0, 0.0)
        place = owner * MOST + jnp.sum(hits, axis=1, keepdims=True)
        code = code + jnp.where(
            place == edge_lane.astype(F32), edge_cols[:, topk + k : topk + k + 1] + 1.0, 0.0
        )
        places = jnp.where(edge_lane == k, place, places)
    codes = jnp.sum(code, axis=0, keepdims=True) - 1.0
    pos_v[...] = places.astype(jnp.int32)
    pos_copy = pltpu.make_async_copy(pos_v, pos_s, pos_sem)
    pos_copy.start()

    def shard_max(ref, h, tiles):
        lanes = slice(h * LANES, (h + 1) * LANES)
        m = ref[lanes, :LANES]
        for t in range(1, tiles):
            m = jnp.maximum(m, ref[lanes, t * LANES : (t + 1) * LANES])
        return jnp.max(m.astype(F32), axis=1, keepdims=True)

    for acc in (acc_lo, acc_hi):
        acc[...] = jnp.full(acc.shape, TINY, F32)
    for h in range(halves):
        x_copy(h).wait()
    teacher_high, teacher_sum = [], []
    for h in range(halves):
        lanes = slice(h * LANES, (h + 1) * LANES)
        high = shard_max(x_ref, h, pairs)
        high_b = jnp.broadcast_to(high, (LANES, LANES))
        total = jnp.zeros((LANES, LANES), F32)
        for q in range(pairs):
            e = jnp.exp2((x_ref[lanes, q * LANES : (q + 1) * LANES].astype(F32) - high_b) * EXP2_SCALE)
            total = total + e
            probs[q, lanes, :] = e.astype(BF16)
        teacher_high.append(high)
        teacher_sum.append(jnp.sum(total, axis=1, keepdims=True))

    y_copy.wait()
    w_copy.wait()
    student_high = [shard_max(y_ref, h, student_tiles) for h in range(halves)]

    pos_copy.wait()

    for h in range(halves):
        high_v[h] = jnp.broadcast_to(student_high[h], (LANES, LANES))
    lane = lax.broadcasted_iota(jnp.int32, (BLK, LANES), 1)
    even = lane % 2 == 0
    first = lane < BLK
    mass = jnp.zeros((8, rows), F32)
    student_total = [jnp.zeros((LANES, LANES), F32) for _ in range(halves)]
    items = [(h, t) for h in range(halves) for t in range(student_tiles)]
    for q in range(pairs):
        w = w_ref[q * LANES : (q + 1) * LANES, :].astype(F32).T
        a0, a1 = w[:BLK], w[BLK:]
        l0 = jnp.where(even, a0, pltpu.roll(a1, 1, 1))
        l1 = jnp.where(even, pltpu.roll(a0, LANES - 1, 1), a1)
        lhs = jnp.concatenate(
            [
                jnp.where(first, l0, 0.0),
                jnp.where(first, l1, 0.0),
                jnp.where(first, 0.0, l0),
                jnp.where(first, 0.0, l1),
            ],
            axis=0,
        ).astype(BF16)
        both = jnp.sum((l0 + l1).reshape(BLK // 8, 8, LANES), axis=0)
        both_hi, both_lo = split2(both)
        lhs = jnp.concatenate([lhs, both_hi.astype(BF16), both_lo.astype(BF16)], axis=0)
        u = lax.dot_general(
            lhs, probs[q], (((1,), (1,)), ((), ())), preferred_element_type=F32
        )
        for h, t in items[len(items) * q // pairs : len(items) * (q + 1) // pairs]:
            y = y_ref[h * LANES : (h + 1) * LANES, t * LANES : (t + 1) * LANES].astype(F32)
            student_total[h] = student_total[h] + jnp.exp2((y - high_v[h]) * EXP2_SCALE)
            yt_ref[h, t * LANES : (t + 1) * LANES, :] = y_ref[
                h * LANES : (h + 1) * LANES, t * LANES : (t + 1) * LANES
            ].T
        mass = mass + u[4 * BLK : 4 * BLK + 8] + u[4 * BLK + 8 :]
        u = u[: 4 * BLK].astype(BF16)
        for edge in range(2 * topk):
            place = pos_s[2 * q + edge // topk, edge % topk]
            at = pl.multiple_of((place % MOST) * block_rows, block_rows)
            for h in range(halves):
                out_ref[place // MOST, pl.ds(at + h * BLK, BLK), :] = u[
                    edge * BLK : (edge + 1) * BLK, h * LANES : (h + 1) * LANES
                ]

    row_lane = lax.broadcasted_iota(jnp.int32, (LANES, LANES), 1)
    r_hi, r_lo = split2(jnp.sum(mass, axis=0, keepdims=True))
    sub = lax.broadcasted_iota(jnp.int32, (8, LANES), 0)
    pieces = []
    for h in range(halves):
        t_hi, t_lo = split2(teacher_sum[h])
        student_sum = jnp.sum(student_total[h], axis=1, keepdims=True)
        s_hi, s_lo = split2(student_high[h] * EXP2_SCALE + jnp.log2(student_sum))
        columns = jnp.zeros((LANES, LANES), F32)
        for i, v in ((0, teacher_high[h]), (1, t_hi), (2, t_lo), (5, s_hi), (6, s_lo)):
            columns = jnp.where(row_lane == i, v, columns)
        lanes = slice(h * LANES, (h + 1) * LANES)
        s = columns.T[:8]
        s = jnp.where(sub == 3, r_hi[:, lanes], s)
        s = jnp.where(sub == 4, r_lo[:, lanes], s)
        pieces.append(jnp.where(sub == CODE_ROW, codes, s))
    stats = jnp.concatenate(pieces, axis=0).astype(BF16)
    for i in range(owners):
        out_ref[i, MOST * block_rows :, :] = stats


def receive_kernel(
    arr_ref, y_ref, lo_in, hi_in, out_hbm, loss_ref, acc_lo, acc_hi, out_ref, wide, scale, code_v, code_s,
    bias, code_sem, out_sem,
):
    owners = arr_ref.shape[0]
    halves, width, _ = y_ref.shape
    tiles = width // LANES
    block_rows = halves * BLK
    accs = (acc_lo, acc_hi)
    vocab_width = float(width * owners)
    me = lax.axis_index("vocab")

    wide[...] = arr_ref[:, MOST * block_rows :, :].astype(F32).reshape(owners * TAIL_ROWS, LANES)
    codes = wide[pl.ds(CODE_ROW, owners, stride=TAIL_ROWS), :].astype(jnp.int32)
    code_v[...] = jnp.where(codes < 0, width // BLK, codes)
    code_copy = pltpu.make_async_copy(code_v, code_s, code_sem)
    code_copy.start()

    row_terms = jnp.zeros((1, LANES), F32)
    for h in range(halves):

        def stat(i):
            return wide[pl.ds(8 * h + i, owners, stride=TAIL_ROWS), :]

        t_high = stat(0)
        t_top = jnp.max(t_high, axis=0, keepdims=True)
        t_rel = jnp.exp2((t_high - t_top) * EXP2_SCALE)
        inv = vocab_width / jnp.sum(t_rel * (stat(1) + stat(2)), axis=0, keepdims=True)
        scale_h = t_rel * inv
        scale[h * owners : (h + 1) * owners, :] = scale_h
        total = jnp.sum(scale_h * (stat(3) + stat(4)), axis=0, keepdims=True)
        log_total = jnp.log2(total)
        s_lse = stat(5) + stat(6)
        s_top = jnp.max(s_lse, axis=0, keepdims=True)
        lse = s_top + jnp.log2(jnp.sum(jnp.exp2(s_lse - s_top), axis=0, keepdims=True))
        bias[h : h + 1, :] = lse - log_total
        row_terms = row_terms + total * (log_total - math.log2(vocab_width)) * (1.0 / owners)

    code_copy.wait()

    def add_source(src, carry):
        for slot in range(MOST):
            c = code_s[src, me * MOST + slot]
            for h in range(halves):
                acc, at = accs[h], pl.ds(pl.multiple_of(c * BLK, BLK), BLK)
                lo = slot * block_rows + h * BLK
                term = arr_ref[src, lo : lo + BLK, :].astype(F32)
                acc[at, :] = acc[at, :] + term * scale[pl.ds(h * owners + src, 1), :]
        return carry

    lax.fori_loop(0, owners, add_source, 0, unroll=8)

    chunks = out_sem.shape[0]
    chunk = width // chunks

    def tile(t, loss):
        cols = pl.ds(pl.multiple_of(t * LANES, LANES), LANES)
        for h in range(halves):
            lanes = slice(h * LANES, (h + 1) * LANES)
            target = accs[h][cols, :]
            goal = y_ref[h, cols, :].astype(F32) * EXP2_SCALE - bias[h : h + 1, :]
            out_ref[lanes, cols] = (jnp.exp2(goal) - target).astype(BF16).T
            term = target * (jnp.log2(target) - goal)
            loss = loss + jnp.sum(term.reshape(LANES // 32, 32, LANES), axis=0)
        return loss

    loss = jnp.zeros((32, LANES), F32)
    out_copies = []
    for i in range(chunks):
        per_chunk = tiles // chunks
        loss = lax.fori_loop(i * per_chunk, (i + 1) * per_chunk, tile, loss, unroll=True)
        part = pl.ds(i * chunk, chunk)
        copy = pltpu.make_async_copy(out_ref.at[:, part], out_hbm.at[:, part], out_sem.at[i])
        copy.start()
        out_copies.append(copy)
    loss_ref[...] = jnp.broadcast_to(
        (jnp.sum(loss, axis=0, keepdims=True) + row_terms).reshape(1, 1, LANES), loss_ref.shape
    )
    for copy in out_copies:
        copy.wait()


def total_kernel(factor, parts_ref, out_ref):
    out_ref[0] = jnp.sum(parts_ref[...]) * factor


def per_device(mentor_score_matrix, learner_score_matrix, align_dev, align_slot, align_weight):
    owners = lax.axis_size("vocab")
    shards = owners * lax.axis_size("dp")
    rows, teacher_width = mentor_score_matrix.shape
    width = learner_score_matrix.shape[1]
    tb_local, topk = align_dev.shape
    halves = rows // LANES
    block_rows = halves * BLK
    packet_rows = MOST * block_rows + TAIL_ROWS
    chunks = BLK * BLK // LANES
    weight = (
        align_weight.reshape(tb_local, topk, chunks, LANES)
        .transpose(0, 2, 1, 3)
        .reshape(tb_local * chunks * topk, LANES)
    )
    vmem = pl.BlockSpec(memory_space=pltpu.VMEM)
    hbm = pl.BlockSpec(memory_space=pltpu.HBM)
    params = pltpu.CompilerParams(vmem_limit_bytes=20 * 2**20)
    acc_shape = (width + BLK, LANES)
    outgoing, learner_t, target_lo, target_hi = pl.pallas_call(
        send_kernel,
        out_shape=(
            jax.ShapeDtypeStruct((owners, packet_rows, LANES), BF16),
            jax.ShapeDtypeStruct((halves, width, LANES), BF16),
            jax.ShapeDtypeStruct(acc_shape, F32),
            jax.ShapeDtypeStruct(acc_shape, F32),
        ),
        in_specs=[hbm] * 5,
        out_specs=(vmem, vmem, vmem, vmem),
        scratch_shapes=[
            pltpu.VMEM((topk, tb_local), jnp.int32),
            pltpu.VMEM((topk, tb_local), jnp.int32),
            pltpu.VMEM((rows, teacher_width), BF16),
            pltpu.VMEM(weight.shape, BF16),
            pltpu.VMEM((rows, width), BF16),
            pltpu.VMEM((teacher_width // LANES, rows, LANES), BF16),
            pltpu.VMEM((halves, LANES, LANES), F32),
            pltpu.VMEM((8, LANES), F32),
            pltpu.VMEM((32, LANES), jnp.int32),
            pltpu.SMEM((32, LANES), jnp.int32),
            pltpu.SemaphoreType.DMA,
            pltpu.SemaphoreType.DMA,
            pltpu.SemaphoreType.DMA,
            pltpu.SemaphoreType.DMA,
            pltpu.SemaphoreType.DMA((halves,)),
            pltpu.SemaphoreType.DMA,
        ],
        compiler_params=params,
        name="send",
    )(*(
        pltpu.with_memory_space_constraint(a, pltpu.HBM)
        for a in (align_dev.T, align_slot.T, mentor_score_matrix, learner_score_matrix, weight)
    ))
    arrived = lax.all_to_all(outgoing, "vocab", split_axis=0, concat_axis=0, tiled=True)
    scaled_grad, loss, _, _ = pl.pallas_call(
        receive_kernel,
        out_shape=(
            jax.ShapeDtypeStruct((rows, width), BF16),
            jax.ShapeDtypeStruct((shards, 1, LANES), F32),
            jax.ShapeDtypeStruct(acc_shape, F32),
            jax.ShapeDtypeStruct(acc_shape, F32),
        ),
        in_specs=[vmem, vmem, vmem, vmem],
        out_specs=(hbm, vmem, vmem, vmem),
        input_output_aliases={2: 2, 3: 3},
        scratch_shapes=[
            pltpu.VMEM((rows, width), BF16),
            pltpu.VMEM((owners * TAIL_ROWS, LANES), F32),
            pltpu.VMEM((halves * owners, LANES), F32),
            pltpu.VMEM((owners, LANES), jnp.int32),
            pltpu.SMEM((owners, LANES), jnp.int32),
            pltpu.VMEM((8, LANES), F32),
            pltpu.SemaphoreType.DMA,
            pltpu.SemaphoreType.DMA((16,)),
        ],
        compiler_params=params,
        name="receive",
    )(arrived, learner_t, target_lo, target_hi)
    parts = lax.all_to_all(loss, ("dp", "vocab"), split_axis=0, concat_axis=0, tiled=True)
    tokens = float(rows * lax.axis_size("dp"))
    unit = math.log(2.0) / (width * owners)
    divergence = pl.pallas_call(
        functools.partial(total_kernel, SMOOTHING_HEAT * SMOOTHING_HEAT * unit / tokens),
        out_shape=jax.ShapeDtypeStruct((1,), F32),
        in_specs=[vmem],
        out_specs=pl.BlockSpec(memory_space=pltpu.SMEM),
        compiler_params=params,
        name="total",
    )(parts).reshape(())
    return scaled_grad, divergence


def solution(mesh):
    in_specs = (
        P("dp", "vocab"),
        P("dp", "vocab"),
        P("vocab", None),
        P("vocab", None),
        P("vocab", None, None),
    )
    out_specs = (P("dp", "vocab"), P())
    return jax.shard_map(
        per_device, mesh=mesh, in_specs=in_specs, out_specs=out_specs, check_vma=False
    )
```
